256 devices in a mesh: tm: 8 (over z), space: 16 (over y, x_hi, core), net: 2 (over x_lo).
Axes of the slice: x: 4 (x_hi: 2, x_lo: 2; x = x_hi * 2 + x_lo), y: 4, z: 8, core: 2. Of those that a mesh axis runs over, the one named last changes fastest.
Arguments:
- query_rows: bfloat16 [2, 8, 32, 64, 2560], P('net', 'tm', 'space'), may hold values from -140 to 140
- key_rows: bfloat16 [2, 8, 32, 64, 2560], P('net', 'tm', 'space'), may hold values from -8 to 8
- value_rows: bfloat16 [2, 8, 32, 64, 2560], P('net', 'tm', 'space'), may hold values from -6 to 6
- time_proj: bfloat16 [2, 256, 2560], P('net'), may hold values from -0.375 to 0.375
- block_list: int32 [8, 32, 9], P('tm', 'space'), may hold values from 0 to 255, as said below
- block_count: int32 [8, 32], P('tm', 'space'), may hold values from 1 to 9
- timestep: int32 [1], replicated, may hold values from 0 to 999
Outputs:
- latent_grad: bfloat16 [8, 32, 64, 2560], P('tm', 'space', None, 'net')
The draws below stay inside these ranges and needn't reach their ends.
Inputs may be any that keep to these rules, and one draw needn't show every extreme that they name: `block_list`: entry (f, b, s) names a block f2 * 32 + b2 with f2 within one of f and b2 within one of b, inside the grid; slot 0 is the query's own block; the first block_count[f, b] entries are distinct; the rest repeat the own block.
All inputs are finite; a program needn't handle non-finite values.
Results may differ from the reference program's by a relative error of at most 0.0053.
Values may be sent and summed in bfloat16 or wider, within the bound.
A program may use at most 64 MiB of HBM per device.

```python
import jax
import jax.numpy as jnp
from jax import lax

HEADS = 20
HD = 128
FREQ = 256
BLK = 64
KSEL = 9
STEPS = 1000
HC = 2560
FRAMES = 8
SBLK = 32


def paired_fields(key):
    base = jax.random.fold_in(key, 41)
    query_key, key_key = jax.random.split(base, 2)
    shape = (2, FRAMES, SBLK, BLK, HEADS * HD)
    queries = jnp.clip(jax.random.normal(query_key, shape, jnp.float32), -6.0, 6.0)
    keyset = jnp.clip(jax.random.normal(key_key, shape, jnp.float32), -6.0, 6.0)
    return (queries, keyset)


def draw_query_rows(key, part):
    return paired_fields(key)[0].astype(jnp.bfloat16)


def draw_key_rows(key, part):
    return paired_fields(key)[1].astype(jnp.bfloat16)


def block_lists(key):
    base = jax.random.fold_in(key, 73)
    rank_key, dense_key, sparse_key = jax.random.split(base, 3)
    frame_step = jnp.array([-1, -1, -1, 0, 0, 1, 1, 1], jnp.int32)
    block_step = jnp.array([-1, 0, 1, -1, 1, -1, 0, 1], jnp.int32)
    frame = jnp.arange(FRAMES, dtype=jnp.int32)[:, None, None]
    block = jnp.arange(SBLK, dtype=jnp.int32)[None, :, None]
    near_frame = frame + frame_step
    near_block = block + block_step
    valid = (near_frame >= 0) & (near_frame < FRAMES) & (near_block >= 0) & (near_block < SBLK)
    ranks = jax.random.randint(rank_key, (FRAMES, SBLK, 8), 0, 1000) * 8 + jnp.arange(8, dtype=jnp.int32)
    ranks = ranks + (1 - valid.astype(jnp.int32)) * 100000
    order = jnp.argsort(ranks, axis=-1)
    chosen = jnp.take_along_axis(near_frame * SBLK + near_block, order, axis=-1)
    own = frame * SBLK + block
    lists = jnp.concatenate([own, chosen[:, :, :KSEL - 1]], axis=-1)
    live_count = jnp.sum(valid.astype(jnp.int32), axis=-1)
    middle = jnp.abs(frame[:, :, 0] - FRAMES // 2) <= FRAMES // 4
    dense = jax.random.randint(dense_key, (FRAMES, SBLK), KSEL - 3, KSEL + 1)
    sparse = jax.random.randint(sparse_key, (FRAMES, SBLK), 1, 4)
    count = jnp.minimum(jnp.where(middle, dense, sparse), 1 + live_count)
    count = count.at[1, 1].set(KSEL)
    slots = jnp.arange(KSEL, dtype=jnp.int32)
    lists = jnp.where(slots[None, None, :] < count[:, :, None], lists, own)
    return (lists.astype(jnp.int32), count.astype(jnp.int32))


def draw_block_list(key, part):
    return block_lists(key)[0]


def draw_block_count(key, part):
    return block_lists(key)[1]


def level_of(own_key, dims, cuts, smallest, top_value):
    level, own = 1.0, jax.random.fold_in(own_key, 6)
    for axis_at, shards_of in cuts:
        heights = jnp.exp(jax.random.uniform(jax.random.fold_in(own, axis_at), (shards_of,), jnp.float32, smallest / len(cuts), top_value / len(cuts)))
        level = level * jnp.repeat(heights, dims[axis_at] // shards_of).reshape([-1 if axis == axis_at else 1 for axis in range(len(dims))])
    return level


def centred(key, shape, width, bound, cuts=(), kind=jnp.bfloat16):
    entries = width * jax.random.normal(key, shape, jnp.float32)
    if cuts:
        entries = entries * level_of(key, shape, cuts, -0.22, 0.18)
    return jnp.clip(entries, -bound, bound).astype(kind)


def setup_inputs(seed: int = 0) -> dict:
    splits = jax.random.split(jax.random.key(seed), 8)
    query_rows = draw_query_rows(jax.random.fold_in(splits[7], 71), 0)
    key_rows = draw_key_rows(jax.random.fold_in(splits[7], 71), 0)
    value_rows = centred(splits[2], (2, FRAMES, SBLK, BLK, HC), 1.0, 6.0, ((0, 2), (1, 8), (2, 16)))
    time_proj = centred(splits[3], (2, FREQ, HC), FREQ ** -0.5, 0.375, ((0, 2),))
    block_list = draw_block_list(jax.random.fold_in(splits[7], 71), 0)
    block_count = draw_block_count(jax.random.fold_in(splits[7], 71), 0)
    timestep = jax.random.randint(splits[6], (1,), 0, STEPS).astype(jnp.int32)
    return dict(query_rows=query_rows, key_rows=key_rows, value_rows=value_rows, time_proj=time_proj, block_list=block_list, block_count=block_count, timestep=timestep)


def attend_network(query_net, key_net, value_net, block_list, block_count):
    key_flat = key_net.reshape(FRAMES * SBLK, BLK, HEADS, HD)
    value_flat = value_net.reshape(FRAMES * SBLK, BLK, HEADS, HD)
    scale = HD ** -0.5

    def one_frame(frame):
        queries = lax.dynamic_index_in_dim(query_net, frame, 0, keepdims=False)
        lists = lax.dynamic_index_in_dim(block_list, frame, 0, keepdims=False)
        counts = lax.dynamic_index_in_dim(block_count, frame, 0, keepdims=False)
        gathered_keys = key_flat[lists].reshape(SBLK, KSEL * BLK, HEADS, HD).astype(jnp.float32)
        gathered_values = value_flat[lists].reshape(SBLK, KSEL * BLK, HEADS, HD).astype(jnp.float32)
        query_heads = queries.reshape(SBLK, BLK, HEADS, HD).astype(jnp.float32)
        scores = jnp.einsum("qihd,qjhd->qhij", query_heads, gathered_keys) * scale
        slots = jnp.arange(KSEL, dtype=jnp.int32)
        live = jnp.repeat(slots[None, :] < counts[:, None], BLK, axis=1)
        scores = jnp.where(live[:, None, None, :], scores, jnp.float32(-1e30))
        top = jnp.max(scores, axis=-1, keepdims=True)
        expo = jnp.where(live[:, None, None, :], jnp.exp(scores - top), jnp.float32(0.0))
        total = jnp.sum(expo, axis=-1)
        weights = expo.astype(jnp.bfloat16).astype(jnp.float32)
        mixed = jnp.einsum("qhij,qjhd->qihd", weights, gathered_values)
        mixed = mixed / jnp.transpose(total, (0, 2, 1))[..., None]
        return mixed.reshape(SBLK, BLK, HEADS * HD)

    return lax.map(one_frame, jnp.arange(FRAMES, dtype=jnp.int32))


def gate_vector(timestep, proj):
    half = FREQ // 2
    freqs = jnp.exp(-jnp.log(jnp.float32(10000.0)) * jnp.arange(half, dtype=jnp.float32) / half)
    angle = timestep[0].astype(jnp.float32) * freqs
    feature = jax.nn.silu(jnp.concatenate([jnp.cos(angle), jnp.sin(angle)])).astype(jnp.bfloat16)
    return jnp.dot(feature[None, :], proj, preferred_element_type=jnp.float32)[0]


def reference(query_rows, key_rows, value_rows, time_proj, block_list, block_count, timestep):
    real_out = attend_network(query_rows[0], key_rows[0], value_rows[0], block_list, block_count)
    fake_out = attend_network(query_rows[1], key_rows[1], value_rows[1], block_list, block_count)
    real_gate = gate_vector(timestep, time_proj[0])
    fake_gate = gate_vector(timestep, time_proj[1])
    return (fake_gate * fake_out - real_gate * real_out).astype(jnp.bfloat16)
```

```python
import functools
import math

import jax
import jax.numpy as jnp
from jax import lax
from jax.experimental import pallas as pl
from jax.experimental.pallas import tpu as pltpu
from jax.sharding import PartitionSpec as P

HD = 128
FREQ = 256
DEAD = -1e30
RATE = HD**-0.5 * math.log2(math.e)
MESH = pl.DeviceIdType.MESH


def kernel(
    chunk,
    block_list,
    block_count,
    timestep,
    q_in,
    k_in,
    v_in,
    proj_in,
    out,
    queries,
    keys,
    values,
    proj,
    gate,
    bias,
    bias_out,
    own_mix,
    own_top,
    own_sum,
    edge_mix,
    edge_stat,
    back_mix,
    back_stat,
    net_out,
    net_in,
    result,
    local_sem,
    result_sem,
    bias_send,
    bias_recv,
    k_send,
    k_recv,
    v_send,
    v_recv,
    q_send,
    q_recv,
    mix_send,
    mix_recv,
    stat_send,
    stat_recv,
    net_send,
    net_recv,
):
    block_len, features = q_in.shape[-2:]
    heads = features // HD
    steps = heads // chunk
    half = steps // 2
    width = chunk * HD
    frames, spaces = lax.axis_size("tm"), lax.axis_size("space")
    frame, space, net = lax.axis_index("tm"), lax.axis_index("space"), lax.axis_index("net")
    up = {"tm": lax.rem(frame + 1, frames)}
    down = {"tm": lax.rem(frame + frames - 1, frames)}
    right = {"space": lax.rem(space + 1, spaces)}
    left = {"space": lax.rem(space + spaces - 1, spaces)}
    other = {"net": 1 - net}

    own_copies = [
        pltpu.make_async_copy(proj_in.at[0], proj, local_sem.at[0]),
        pltpu.make_async_copy(q_in.at[0, 0], queries.at[pl.ds(1, 2)], local_sem.at[1]),
        pltpu.make_async_copy(k_in.at[0, 0], keys.at[1], local_sem.at[2]),
        pltpu.make_async_copy(v_in.at[0, 0], values.at[1], local_sem.at[3]),
    ]
    for copy in own_copies:
        copy.start()

    barrier = pltpu.get_barrier_semaphore()
    for peer in (up, down, left, right, other):
        pl.semaphore_signal(barrier, inc=1, device_id=peer, device_id_type=MESH)
    pl.semaphore_wait(barrier, 5)

    def send(src, dst, send_sem, recv_sem, peer):
        return pltpu.make_async_remote_copy(
            src_ref=src,
            dst_ref=dst,
            send_sem=send_sem,
            recv_sem=recv_sem,
            device_id=peer,
            device_id_type=MESH,
        )

    def lanes(step):
        first = lax.rem((1 - net) * (heads // 2) + step * chunk, heads)
        return pl.ds(pl.multiple_of(first * HD, HD), width)

    def half_lanes(step):
        return pl.ds(pl.multiple_of(step * width, HD), width)

    def arrivals(step):
        at = lanes(step)
        copies = []
        for way, peer, slot in ((0, up, 0), (1, down, 2)):
            copies.append(
                send(
                    k_in.at[0, 0, :, :, at],
                    keys.at[slot, :, :, at],
                    k_send.at[step, way],
                    k_recv.at[step, way],
                    peer,
                )
            )
            copies.append(
                send(
                    v_in.at[0, 0, :, :, at],
                    values.at[slot, :, :, at],
                    v_send.at[step, way],
                    v_recv.at[step, way],
                    peer,
                )
            )
        for way, peer, slot in ((0, left, 3), (1, right, 0)):
            copies.append(
                send(
                    q_in.at[0, 0, way, :, at],
                    queries.at[slot, :, at],
                    q_send.at[step, way],
                    q_recv.at[step, way],
                    peer,
                )
            )
        return copies

    def returns(step):
        at = lanes(step)
        copies = []
        for edge, peer in ((0, left), (1, right)):
            copies.append(
                send(
                    edge_mix.at[edge, :, at],
                    back_mix.at[1 - edge, :, at],
                    mix_send.at[step, edge],
                    mix_recv.at[step, edge],
                    peer,
                )
            )
            copies.append(
                send(
                    edge_stat.at[step, edge],
                    back_stat.at[step, 1 - edge],
                    stat_send.at[step, edge],
                    stat_recv.at[step, edge],
                    peer,
                )
            )
        return copies

    def crossing(step):
        at = half_lanes(step)
        return send(
            net_out.at[:, at], net_in.at[:, at], net_send.at[step], net_recv.at[step], other
        )

    def leaving(step):
        at = half_lanes(step)
        return pltpu.make_async_copy(
            result.at[:, :, at], out.at[0, :, :, at], result_sem.at[step]
        )

    @pl.loop(0, steps)
    def _(step):
        for copy in arrivals(step):
            copy.start()

    column = lax.broadcasted_iota(jnp.int32, (8, 6 * block_len), 1) // block_len
    slots = block_list.shape[-1]

    def listed(row, frame_step, block_step):
        total = 2 * spaces
        wanted = (frame + frame_step) * total + 2 * space + row + block_step
        found = jnp.int32(0)
        for slot in range(slots):
            hit = (block_list[0, row, slot] == wanted) & (slot < block_count[0, row])
            found = found | hit.astype(jnp.int32)
        return jnp.where(found > 0, jnp.float32(0.0), jnp.float32(DEAD))

    def bias_row(entries):
        row = jnp.full(column.shape, DEAD, jnp.float32)
        for place, entry in entries:
            row = jnp.where(column == place, entry, row)
        return row

    for row in range(2):
        bias[1 + row] = bias_row(
            [
                (2 * f + b, listed(row, f - 1, b - row))
                for f in range(3)
                for b in range(2)
            ]
        )
    bias_out[0] = bias_row([(2 * f + 1, listed(0, f - 1, -1)) for f in range(3)])
    bias_out[1] = bias_row([(2 * f, listed(1, f - 1, 1)) for f in range(3)])
    bias_copies = [
        send(bias_out.at[0], bias.at[3], bias_send.at[0], bias_recv.at[0], left),
        send(bias_out.at[1], bias.at[0], bias_send.at[1], bias_recv.at[1], right),
    ]
    for copy in bias_copies:
        copy.start()

    order = lax.broadcasted_iota(jnp.int32, (8, FREQ // 2), 1).astype(jnp.float32)
    rates = jnp.exp(-jnp.log(jnp.full_like(order, 10000.0)) * order / (FREQ // 2))
    angle = timestep[0].astype(jnp.float32) * rates
    feature = jnp.concatenate([jnp.cos(angle), jnp.sin(angle)], axis=1)
    feature = (feature / (1.0 + jnp.exp(-feature))).astype(jnp.bfloat16)
    polarity = 2.0 * net.astype(jnp.float32) - 1.0
    for copy in own_copies:
        copy.wait()

    @pl.loop(0, heads)
    def _(head):
        at = pl.ds(pl.multiple_of(head * HD, HD), HD)
        gate[:, at] = polarity * jnp.dot(
            feature, proj[:, at], preferred_element_type=jnp.float32
        )

    for copy in bias_copies:
        copy.wait()

    rows = 2 * block_len

    def attend(step):
        for copy in arrivals(step):
            copy.wait_recv()
        start = lanes(step).start
        for j in range(chunk):
            at = pl.ds(pl.multiple_of(start + j * HD, HD), HD)
            q = queries[:, :, at].reshape(4 * block_len, HD)
            k = keys[:, :, :, at].reshape(6 * block_len, HD)
            v = values[:, :, :, at].reshape(6 * block_len, HD)
            scores = lax.dot_general(
                q, k, (((1,), (1,)), ((), ())), preferred_element_type=jnp.float32
            )
            scores = scores.reshape(4, block_len // 8, 8, 6 * block_len) + bias[...][:, None]
            scores = scores.reshape(4 * block_len, 6 * block_len)
            top = jnp.max(scores, axis=-1, keepdims=True)
            expo = jnp.exp2((scores - top) * RATE)
            total = jnp.sum(expo, axis=-1, keepdims=True)
            mix = jnp.dot(expo.astype(jnp.bfloat16), v, preferred_element_type=jnp.float32)
            edge_mix[0, :, at] = mix[:block_len].astype(jnp.bfloat16)
            edge_mix[1, :, at] = mix[3 * block_len :].astype(jnp.bfloat16)
            edge_stat[step, 0, :, j : j + 1] = top[:block_len]
            edge_stat[step, 1, :, j : j + 1] = top[3 * block_len :]
            edge_stat[step, 0, :, 64 + j : 65 + j] = total[:block_len]
            edge_stat[step, 1, :, 64 + j : 65 + j] = total[3 * block_len :]
            own_mix[:, at] = mix[block_len : 3 * block_len]
            own_top[step, j] = top[block_len : 3 * block_len]
            own_sum[step, j] = total[block_len : 3 * block_len]
        for copy in returns(step):
            copy.start()

    def combine(step):
        for copy in returns(step):
            copy.wait_recv()
        start = lanes(step).start

        def term(j):
            at = pl.ds(pl.multiple_of(start + j * HD, HD), HD)
            stat = back_stat[step].reshape(rows, HD)
            top, more_top = own_top[step, j], stat[:, j : j + 1]
            total, more_total = own_sum[step, j], stat[:, 64 + j : 65 + j]
            new_top = jnp.maximum(top, more_top)
            keep = jnp.exp2((top - new_top) * RATE)
            more = jnp.exp2((more_top - new_top) * RATE)
            whole = keep * total + more * more_total
            mixed = own_mix[:, at] * (keep / whole) + back_mix[:, :, at].reshape(
                rows, HD
            ).astype(jnp.float32) * (more / whole)
            gates = gate[:, at]
            return (mixed.reshape(rows // 8, 8, HD) * gates[None]).reshape(rows, HD)

        @pl.when(step < half)
        def _():
            for j in range(chunk):
                at = pl.ds(pl.multiple_of(step * width + j * HD, HD), HD)
                net_out[:, at] = term(j).astype(jnp.bfloat16)
            crossing(step).start()

        @pl.when(step >= half)
        def _():
            crossing(step - half).wait_recv()
            for j in range(chunk):
                at = pl.ds(pl.multiple_of((step - half) * width + j * HD, HD), HD)
                full = term(j) + net_in[:, at].astype(jnp.float32)
                result[:, :, at] = full.astype(jnp.bfloat16).reshape(2, block_len, HD)
            leaving(step - half).start()

    @pl.loop(0, steps)
    def _(step):
        attend(step)

        @pl.when(step > 0)
        def _():
            combine(step - 1)

    combine(steps - 1)

    @pl.loop(0, steps)
    def _(step):
        for copy in arrivals(step):
            copy.wait_send()
        for copy in returns(step):
            copy.wait_send()

    @pl.loop(0, half)
    def _(step):
        crossing(step).wait_send()
        leaving(step).wait()


def shards(query_rows, key_rows, value_rows, time_proj, block_list, block_count, timestep, *, chunk):
    block_len, features = query_rows.shape[-2:]
    heads = features // HD
    steps = heads // chunk
    bf16, f32 = jnp.bfloat16, jnp.float32
    vmem, dma = pltpu.VMEM, pltpu.SemaphoreType.DMA
    smem = pl.BlockSpec(memory_space=pltpu.SMEM)
    hbm = pl.BlockSpec(memory_space=pltpu.HBM)
    return pl.pallas_call(
        functools.partial(kernel, chunk),
        out_shape=jax.ShapeDtypeStruct((1, 2, block_len, features // 2), bf16),
        in_specs=[smem, smem, smem, hbm, hbm, hbm, hbm],
        out_specs=hbm,
        scratch_shapes=[
            vmem((4, block_len, features), bf16),
            vmem((3, 2, block_len, features), bf16),
            vmem((3, 2, block_len, features), bf16),
            vmem((FREQ, features), bf16),
            vmem((8, features), f32),
            vmem((4, 8, 6 * block_len), f32),
            vmem((2, 8, 6 * block_len), f32),
            vmem((2 * block_len, features), f32),
            vmem((steps, chunk, 2 * block_len, 1), f32),
            vmem((steps, chunk, 2 * block_len, 1), f32),
            vmem((2, block_len, features), bf16),
            vmem((steps, 2, block_len, HD), f32),
            vmem((2, block_len, features), bf16),
            vmem((steps, 2, block_len, HD), f32),
            vmem((2 * block_len, features // 2), bf16),
            vmem((2 * block_len, features // 2), bf16),
            vmem((2, block_len, features // 2), bf16),
            dma((4,)),
            dma((steps // 2,)),
            dma((2,)),
            dma((2,)),
            dma((steps, 2)),
            dma((steps, 2)),
            dma((steps, 2)),
            dma((steps, 2)),
            dma((steps, 2)),
            dma((steps, 2)),
            dma((steps, 2)),
            dma((steps, 2)),
            dma((steps, 2)),
            dma((steps, 2)),
            dma((steps // 2,)),
            dma((steps // 2,)),
        ],
        compiler_params=pltpu.CompilerParams(
            collective_id=0, has_side_effects=True, vmem_limit_bytes=60 << 20
        ),
        name="radial_attention",
    )(block_list, block_count, timestep, query_rows, key_rows, value_rows, time_proj)


def solution(mesh, chunk=5):
    return jax.shard_map(
        functools.partial(shards, chunk=chunk),
        mesh=mesh,
        in_specs=(
            P("net", "tm", "space", None, None),
            P("net", "tm", "space", None, None),
            P("net", "tm", "space", None, None),
            P("net", None, None),
            P("tm", "space", None),
            P("tm", "space"),
            P(),
        ),
        out_specs=P("tm", "space", None, "net"),
        check_vma=False,
    )
```

```python
import functools
import math

import jax
import jax.numpy as jnp
from jax import lax
from jax.experimental import pallas as pl
from jax.experimental.pallas import tpu as pltpu
from jax.sharding import PartitionSpec as P

HD = 128
FREQ = 256
DEAD = -1e30
RATE = HD**-0.5 * math.log2(math.e)
MESH = pl.DeviceIdType.MESH


def kernel(
    chunk,
    block_list,
    block_count,
    timestep,
    q_in,
    k_in,
    v_in,
    proj_in,
    out,
    queries,
    keys,
    values,
    proj,
    gate,
    bias,
    bias_in,
    bias_out,
    own_mix,
    own_top,
    own_sum,
    columns,
    far_mix,
    far_stat,
    back_mix,
    back_stat,
    net_out,
    net_in,
    result,
    local_sem,
    result_sem,
    bias_send,
    bias_recv,
    q_send,
    q_recv,
    k_send,
    k_recv,
    v_send,
    v_recv,
    mix_send,
    mix_recv,
    stat_send,
    stat_recv,
    net_send,
    net_recv,
):
    block_len, features = q_in.shape[-2:]
    heads = features // HD
    steps = heads // chunk
    half = steps // 2
    width = chunk * HD
    rows = 2 * block_len
    frames, spaces = lax.axis_size("tm"), lax.axis_size("space")
    frame, space, net = lax.axis_index("tm"), lax.axis_index("space"), lax.axis_index("net")
    down, has_down = {"tm": frame - 1}, frame > 0
    up, has_up = {"tm": frame + 1}, frame < frames - 1
    left, has_left = {"space": space - 1}, space > 0
    right, has_right = {"space": space + 1}, space < spaces - 1
    other = {"net": 1 - net}

    barrier = pltpu.get_barrier_semaphore()
    peers = ((down, has_down), (up, has_up), (left, has_left), (right, has_right))
    for peer, there in peers:

        @pl.when(there)
        def _():
            pl.semaphore_signal(barrier, inc=1, device_id=peer, device_id_type=MESH)

    pl.semaphore_signal(barrier, inc=1, device_id=other, device_id_type=MESH)

    own_copies = [
        pltpu.make_async_copy(q_in.at[0, 0], queries.at[pl.ds(2, 2)], local_sem.at[0]),
        pltpu.make_async_copy(k_in.at[0, 0], keys.at[pl.ds(1, 2)], local_sem.at[1]),
        pltpu.make_async_copy(v_in.at[0, 0], values.at[pl.ds(1, 2)], local_sem.at[2]),
        pltpu.make_async_copy(proj_in.at[0], proj, local_sem.at[3]),
    ]
    for copy in own_copies:
        copy.start()

    column = lax.broadcasted_iota(jnp.int32, (8, 4 * block_len), 1) // block_len
    sublane = lax.broadcasted_iota(jnp.int32, (8, 4 * block_len), 0)
    slots = block_list.shape[-1]

    def listed(row, frame_step, block_step):
        wanted = (frame + frame_step) * (2 * spaces) + 2 * space + row + block_step
        found = jnp.int32(0)
        for slot in range(slots):
            hit = (block_list[0, row, slot] == wanted) & (slot < block_count[0, row])
            found = found | hit.astype(jnp.int32)
        return jnp.where(found > 0, jnp.float32(0.0), jnp.float32(DEAD))

    def bias_rows(frame_step):
        both = []
        for row in range(2):
            entries = jnp.full(column.shape, DEAD, jnp.float32)
            for place in range(row, row + 3):
                entry = listed(row, frame_step, place - 1 - row)
                entries = jnp.where(column == place, entry, entries)
            both.append(entries)
        return jnp.where(sublane == 0, both[0], both[1])

    bias_out[0] = bias_rows(-1)
    bias_out[1] = bias_rows(1)
    bias_in[1] = bias_rows(0)

    pl.semaphore_wait(barrier, 1 + sum(there.astype(jnp.int32) for _, there in peers))

    def send(src, dst, send_sem, recv_sem, peer):
        return pltpu.make_async_remote_copy(
            src_ref=src,
            dst_ref=dst,
            send_sem=send_sem,
            recv_sem=recv_sem,
            device_id=peer,
            device_id_type=MESH,
        )

    def lanes(step):
        first = lax.rem((1 - net) * (heads // 2) + step * chunk, heads)
        return pl.ds(pl.multiple_of(first * HD, HD), width)

    def half_lanes(step):
        return pl.ds(pl.multiple_of(step * width, HD), width)

    over_z = ((0, down, 2, has_down, has_up), (1, up, 0, has_up, has_down))
    over_space = ((0, left, 3, has_left, has_right), (1, right, 0, has_right, has_left))

    def bias_copies():
        return [
            (
                send(
                    bias_out.at[way], bias_in.at[group], bias_send.at[way], bias_recv.at[way], peer
                ),
                sends,
                receives,
            )
            for way, peer, group, sends, receives in over_z
        ]

    def streams(step):
        at = lanes(step)
        copies = []
        for way, peer, group, sends, receives in over_z:
            copy = send(
                q_in.at[0, 0, :, :, at],
                queries.at[pl.ds(2 * group, 2), :, at],
                q_send.at[step, way],
                q_recv.at[step, way],
                peer,
            )
            copies.append((copy, sends, receives))
        for source, kept, send_sem, recv_sem in (
            (k_in, keys, k_send, k_recv),
            (v_in, values, v_send, v_recv),
        ):
            for way, peer, place, sends, receives in over_space:
                copy = send(
                    source.at[0, 0, way, :, at],
                    kept.at[place, :, at],
                    send_sem.at[step, way],
                    recv_sem.at[step, way],
                    peer,
                )
                copies.append((copy, sends, receives))
        return copies

    def returns(step):
        at = lanes(step)
        copies = []
        for way, peer, _, sends, receives in over_z:
            stat = send(
                far_stat.at[step, way],
                back_stat.at[step, 1 - way],
                stat_send.at[step, way],
                stat_recv.at[step, way],
                peer,
            )
            mix = send(
                far_mix.at[way, :, at],
                back_mix.at[1 - way, :, at],
                mix_send.at[step, way],
                mix_recv.at[step, way],
                peer,
            )
            copies += [(stat, sends, receives), (mix, sends, receives)]
        return copies

    def crossing(step):
        at = half_lanes(step)
        return send(
            net_out.at[:, at], net_in.at[:, at], net_send.at[step], net_recv.at[step], other
        )

    def leaving(step):
        at = half_lanes(step)
        return pltpu.make_async_copy(
            result.at[:, :, at], out.at[0, :, :, at], result_sem.at[step]
        )

    def start_all(copies):
        for copy, sends, _ in copies:
            pl.when(sends)(copy.start)

    def receive_all(copies):
        for copy, _, receives in copies:
            pl.when(receives)(copy.wait_recv)

    def sent_all(copies):
        for copy, sends, _ in copies:
            pl.when(sends)(copy.wait_send)

    start_all(bias_copies())

    @pl.loop(0, steps)
    def _(step):
        start_all(streams(step))

    def edge_copies(block, place):
        return [
            pltpu.make_async_copy(k_in.at[0, 0, block], keys.at[place], local_sem.at[4 + block]),
            pltpu.make_async_copy(v_in.at[0, 0, block], values.at[place], local_sem.at[6 + block]),
        ]

    edges = ((has_left, 0, 0), (has_right, 1, 3))
    for there, block, place in edges:

        @pl.when(jnp.logical_not(there))
        def _():
            for copy in edge_copies(block, place):
                copy.start()

    for there, way in ((has_down, 0), (has_up, 1)):

        @pl.when(jnp.logical_not(there))
        def _():
            for block in range(2):
                queries[4 * way + block] = jnp.zeros((block_len, features), queries.dtype)
            bias_in[2 * way] = jnp.full(bias_in.shape[1:], DEAD, jnp.float32)
            back_mix[way] = jnp.zeros(back_mix.shape[1:], back_mix.dtype)
            kind = lax.broadcasted_iota(jnp.int32, back_stat.shape[2:], 0)
            for step in range(steps):
                back_stat[step, way] = jnp.where(kind < 8, DEAD, 0.0)

    order = lax.broadcasted_iota(jnp.int32, (8, FREQ // 2), 1).astype(jnp.float32)
    rates = jnp.exp(-jnp.log(jnp.full_like(order, 10000.0)) * order / (FREQ // 2))
    angle = timestep[0].astype(jnp.float32) * rates
    feature = jnp.concatenate([jnp.cos(angle), jnp.sin(angle)], axis=1)
    feature = (feature / (1.0 + jnp.exp(-feature))).astype(jnp.bfloat16)
    polarity = 2.0 * net.astype(jnp.float32) - 1.0
    for copy in own_copies:
        copy.wait()
    for there, block, place in edges:

        @pl.when(jnp.logical_not(there))
        def _():
            for copy in edge_copies(block, place):
                copy.wait()

    @pl.loop(0, heads)
    def _(head):
        at = pl.ds(pl.multiple_of(head * HD, HD), HD)
        gate[:, at] = polarity * jnp.dot(
            feature, proj[:, at], preferred_element_type=jnp.float32
        )

    columns[...] = jnp.zeros_like(columns)
    receive_all(bias_copies())
    for group in range(3):
        for row in range(2):
            bias[2 * group + row] = jnp.broadcast_to(
                bias_in[group, row : row + 1, :], bias.shape[1:]
            )

    @pl.loop(0, steps)
    def _(step):
        receive_all(streams(step))
        start = lanes(step).start
        for j in range(chunk):
            at = pl.ds(pl.multiple_of(start + j * HD, HD), HD)
            q = queries[:, :, at].reshape(6 * block_len, HD)
            k = keys[:, :, at].reshape(4 * block_len, HD)
            v = values[:, :, at].reshape(4 * block_len, HD)
            scores = lax.dot_general(
                q, k, (((1,), (1,)), ((), ())), preferred_element_type=jnp.float32
            )
            scores = scores.reshape(6, block_len // 8, 8, 4 * block_len) + bias[...][:, None]
            scores = scores.reshape(6 * block_len, 4 * block_len)
            top = jnp.max(scores, axis=-1, keepdims=True)
            expo = jnp.exp2((scores - top) * RATE)
            total = jnp.sum(expo, axis=-1, keepdims=True)
            mix = jnp.dot(expo.astype(jnp.bfloat16), v, preferred_element_type=jnp.float32)
            for way in range(2):
                far = slice(2 * way * rows, (2 * way + 1) * rows)
                far_mix[way, :, at] = mix[far].astype(jnp.bfloat16)
                columns[way, :, j : j + 1] = top[far]
                columns[way, :, 8 + j : 9 + j] = total[far]
            own_mix[:, at] = mix[rows : 2 * rows]
            own_top[step, j] = top[rows : 2 * rows]
            own_sum[step, j] = total[rows : 2 * rows]
        for way in range(2):
            far_stat[step, way] = columns[way].T[:16]
        start_all(returns(step))

    def combine(step):
        receive_all(returns(step))
        start = lanes(step).start
        stat = back_stat[step].reshape(32, rows)
        stat = jnp.concatenate([stat, jnp.zeros((HD - 32, rows), jnp.float32)], axis=0).T

        def term(j):
            at = pl.ds(pl.multiple_of(start + j * HD, HD), HD)
            tops = [own_top[step, j], stat[:, j : j + 1], stat[:, 16 + j : 17 + j]]
            sums = [own_sum[step, j], stat[:, 8 + j : 9 + j], stat[:, 24 + j : 25 + j]]
            mixes = [own_mix[:, at]] + [back_mix[way, :, at].astype(jnp.float32) for way in (0, 1)]
            top = jnp.maximum(jnp.maximum(tops[0], tops[1]), tops[2])
            scales = [jnp.exp2((t - top) * RATE) for t in tops]
            whole = 1.0 / sum(a * b for a, b in zip(scales, sums))
            mixed = sum(a * (b * whole) for a, b in zip(mixes, scales))
            return (mixed.reshape(rows // 8, 8, HD) * gate[:, at][None]).reshape(rows, HD)

        @pl.when(step < half)
        def _():
            for j in range(chunk):
                at = pl.ds(pl.multiple_of(step * width + j * HD, HD), HD)
                net_out[:, at] = term(j).astype(jnp.bfloat16)
            crossing(step).start()

        @pl.when(step >= half)
        def _():
            crossing(step - half).wait_recv()
            for j in range(chunk):
                at = pl.ds(pl.multiple_of((step - half) * width + j * HD, HD), HD)
                full = term(j) + net_in[:, at].astype(jnp.float32)
                result[:, :, at] = full.astype(jnp.bfloat16).reshape(2, block_len, HD)
            leaving(step - half).start()

    pl.loop(0, steps)(combine)

    sent_all(bias_copies())

    @pl.loop(0, steps)
    def _(step):
        sent_all(streams(step))
        sent_all(returns(step))

    @pl.loop(0, half)
    def _(step):
        crossing(step).wait_send()
        leaving(step).wait()


def shards(query_rows, key_rows, value_rows, time_proj, block_list, block_count, timestep, *, chunk):
    block_len, features = query_rows.shape[-2:]
    heads = features // HD
    steps = heads // chunk
    rows = 2 * block_len
    bf16, f32 = jnp.bfloat16, jnp.float32
    vmem, dma = pltpu.VMEM, pltpu.SemaphoreType.DMA
    smem = pl.BlockSpec(memory_space=pltpu.SMEM)
    hbm = pl.BlockSpec(memory_space=pltpu.HBM)
    pairs = [dma((steps, 2))] * 2
    return pl.pallas_call(
        functools.partial(kernel, chunk),
        out_shape=jax.ShapeDtypeStruct((1, 2, block_len, features // 2), bf16),
        in_specs=[smem, smem, smem, hbm, hbm, hbm, hbm],
        out_specs=hbm,
        scratch_shapes=[
            vmem((6, block_len, features), bf16),
            vmem((4, block_len, features), bf16),
            vmem((4, block_len, features), bf16),
            vmem((FREQ, features), bf16),
            vmem((8, features), f32),
            vmem((6, 8, 4 * block_len), f32),
            vmem((3, 8, 4 * block_len), f32),
            vmem((2, 8, 4 * block_len), f32),
            vmem((rows, features), f32),
            vmem((steps, chunk, rows, 1), f32),
            vmem((steps, chunk, rows, 1), f32),
            vmem((2, rows, HD), f32),
            vmem((2, rows, features), bf16),
            vmem((steps, 2, 16, rows), f32),
            vmem((2, rows, features), bf16),
            vmem((steps, 2, 16, rows), f32),
            vmem((rows, features // 2), bf16),
            vmem((rows, features // 2), bf16),
            vmem((2, block_len, features // 2), bf16),
            dma((8,)),
            dma((steps // 2,)),
            *([dma((2,))] * 2),
            *pairs,
            *pairs,
            *pairs,
            *pairs,
            *pairs,
            *([dma((steps // 2,))] * 2),
        ],
        compiler_params=pltpu.CompilerParams(
            collective_id=0, has_side_effects=True, vmem_limit_bytes=60 << 20
        ),
        name="radial_attention",
    )(block_list, block_count, timestep, query_rows, key_rows, value_rows, time_proj)


def solution(mesh, chunk=5):
    return jax.shard_map(
        functools.partial(shards, chunk=chunk),
        mesh=mesh,
        in_specs=(
            P("net", "tm", "space", None, None),
            P("net", "tm", "space", None, None),
            P("net", "tm", "space", None, None),
            P("net", None, None),
            P("tm", "space", None),
            P("tm", "space"),
            P(),
        ),
        out_specs=P("tm", "space", None, "net"),
        check_vma=False,
    )
```

```python
import functools
import math

import jax
import jax.numpy as jnp
from jax import lax
from jax.experimental import pallas as pl
from jax.experimental.pallas import tpu as pltpu
from jax.sharding import PartitionSpec as P

HD = 128
FREQ = 256
DEAD = -1e30
RATE = HD**-0.5 * math.log2(math.e)
MESH = pl.DeviceIdType.MESH


def kernel(
    chunk,
    list_in,
    count_in,
    time_in,
    q_in,
    k_in,
    v_in,
    proj_in,
    out,
    block_list,
    block_count,
    timestep,
    queries,
    keys,
    values,
    proj,
    gate,
    bias,
    bias_in,
    bias_out,
    own_mix,
    own_top,
    own_sum,
    columns,
    far_mix,
    far_stat,
    back_mix,
    back_stat,
    net_out,
    net_in,
    local_sem,
    bias_send,
    bias_recv,
    q_send,
    q_recv,
    k_send,
    k_recv,
    v_send,
    v_recv,
    mix_send,
    mix_recv,
    stat_send,
    stat_recv,
    net_send,
    net_recv,
):
    block_len, features = q_in.shape[-2:]
    heads = features // HD
    steps = heads // chunk
    half = steps // 2
    width = chunk * HD
    rows = 2 * block_len
    frames, spaces = lax.axis_size("tm"), lax.axis_size("space")
    frame, space, net = lax.axis_index("tm"), lax.axis_index("space"), lax.axis_index("net")
    down, has_down = {"tm": frame - 1}, frame > 0
    up, has_up = {"tm": frame + 1}, frame < frames - 1
    left, has_left = {"space": space - 1}, space > 0
    right, has_right = {"space": space + 1}, space < spaces - 1
    other = {"net": 1 - net}

    barrier = pltpu.get_barrier_semaphore()
    peers = ((down, has_down), (up, has_up), (left, has_left), (right, has_right))
    for peer, there in peers:

        @pl.when(there)
        def _():
            pl.semaphore_signal(barrier, inc=1, device_id=peer, device_id_type=MESH)

    pl.semaphore_signal(barrier, inc=1, device_id=other, device_id_type=MESH)

    tables = [
        pltpu.make_async_copy(list_in, block_list, local_sem.at[8]),
        pltpu.make_async_copy(count_in, block_count, local_sem.at[9]),
        pltpu.make_async_copy(time_in, timestep, local_sem.at[10]),
    ]
    for copy in tables:
        copy.start()
    own_copies = [
        pltpu.make_async_copy(q_in.at[0, 0], queries.at[pl.ds(2, 2)], local_sem.at[0]),
        pltpu.make_async_copy(k_in.at[0, 0], keys.at[pl.ds(1, 2)], local_sem.at[1]),
        pltpu.make_async_copy(v_in.at[0, 0], values.at[pl.ds(1, 2)], local_sem.at[2]),
        pltpu.make_async_copy(proj_in.at[0], proj, local_sem.at[3]),
    ]
    for copy in own_copies:
        copy.start()

    for copy in tables:
        copy.wait()

    column = lax.broadcasted_iota(jnp.int32, (8, 4 * block_len), 1) // block_len
    sublane = lax.broadcasted_iota(jnp.int32, (8, 4 * block_len), 0)
    slots = block_list.shape[-1]

    def listed(row, frame_step, block_step):
        wanted = (frame + frame_step) * (2 * spaces) + 2 * space + row + block_step
        found = jnp.int32(0)
        for slot in range(slots):
            hit = (block_list[0, row, slot] == wanted) & (slot < block_count[0, row])
            found = found | hit.astype(jnp.int32)
        return jnp.where(found > 0, jnp.float32(0.0), jnp.float32(DEAD))

    def bias_rows(frame_step):
        both = []
        for row in range(2):
            entries = jnp.full(column.shape, DEAD, jnp.float32)
            for place in range(row, row + 3):
                entry = listed(row, frame_step, place - 1 - row)
                entries = jnp.where(column == place, entry, entries)
            both.append(entries)
        return jnp.where(sublane == 0, both[0], both[1])

    bias_out[0] = bias_rows(-1)
    bias_out[1] = bias_rows(1)
    bias_in[1] = bias_rows(0)

    pl.semaphore_wait(barrier, 1 + sum(there.astype(jnp.int32) for _, there in peers))

    def send(src, dst, send_sem, recv_sem, peer):
        return pltpu.make_async_remote_copy(
            src_ref=src,
            dst_ref=dst,
            send_sem=send_sem,
            recv_sem=recv_sem,
            device_id=peer,
            device_id_type=MESH,
        )

    def lanes(step):
        first = lax.rem((1 - net) * (heads // 2) + step * chunk, heads)
        return pl.ds(pl.multiple_of(first * HD, HD), width)

    def half_lanes(step):
        return pl.ds(pl.multiple_of(step * width, HD), width)

    over_z = ((0, down, 2, has_down, has_up), (1, up, 0, has_up, has_down))
    over_space = ((0, left, 3, has_left, has_right), (1, right, 0, has_right, has_left))

    def bias_copies():
        return [
            (
                send(
                    bias_out.at[way], bias_in.at[group], bias_send.at[way], bias_recv.at[way], peer
                ),
                sends,
                receives,
            )
            for way, peer, group, sends, receives in over_z
        ]

    def streams(step):
        at = lanes(step)
        copies = []
        for way, peer, group, sends, receives in over_z:
            copy = send(
                q_in.at[0, 0, :, :, at],
                queries.at[pl.ds(2 * group, 2), :, at],
                q_send.at[step, way],
                q_recv.at[step, way],
                peer,
            )
            copies.append((copy, sends, receives))
        for source, kept, send_sem, recv_sem in (
            (k_in, keys, k_send, k_recv),
            (v_in, values, v_send, v_recv),
        ):
            for way, peer, place, sends, receives in over_space:
                copy = send(
                    source.at[0, 0, way, :, at],
                    kept.at[place, :, at],
                    send_sem.at[step, way],
                    recv_sem.at[step, way],
                    peer,
                )
                copies.append((copy, sends, receives))
        return copies

    def returns(step):
        at = lanes(step)
        copies = []
        for way, peer, _, sends, receives in over_z:
            stat = send(
                far_stat.at[step, way],
                back_stat.at[step, 1 - way],
                stat_send.at[step, way],
                stat_recv.at[step, way],
                peer,
            )
            mix = send(
                far_mix.at[way, :, at],
                back_mix.at[1 - way, :, at],
                mix_send.at[step, way],
                mix_recv.at[step, way],
                peer,
            )
            copies += [(stat, sends, receives), (mix, sends, receives)]
        return copies

    def crossing(step):
        at = half_lanes(step)
        return send(
            net_out.at[:, at], net_in.at[:, at], net_send.at[step], net_recv.at[step], other
        )

    def start_all(copies):
        for copy, sends, _ in copies:
            pl.when(sends)(copy.start)

    def receive_all(copies):
        for copy, _, receives in copies:
            pl.when(receives)(copy.wait_recv)

    def sent_all(copies):
        for copy, sends, _ in copies:
            pl.when(sends)(copy.wait_send)

    start_all(bias_copies())

    @pl.loop(0, steps)
    def _(step):
        start_all(streams(step))

    def edge_copies(block, place):
        return [
            pltpu.make_async_copy(k_in.at[0, 0, block], keys.at[place], local_sem.at[4 + block]),
            pltpu.make_async_copy(v_in.at[0, 0, block], values.at[place], local_sem.at[6 + block]),
        ]

    edges = ((has_left, 0, 0), (has_right, 1, 3))
    for there, block, place in edges:

        @pl.when(jnp.logical_not(there))
        def _():
            for copy in edge_copies(block, place):
                copy.start()

    for there, way in ((has_down, 0), (has_up, 1)):

        @pl.when(jnp.logical_not(there))
        def _():
            for block in range(2):
                queries[4 * way + block] = jnp.zeros((block_len, features), queries.dtype)
            bias_in[2 * way] = jnp.full(bias_in.shape[1:], DEAD, jnp.float32)
            back_mix[way] = jnp.zeros(back_mix.shape[1:], back_mix.dtype)
            kind = lax.broadcasted_iota(jnp.int32, back_stat.shape[2:], 0)
            for step in range(steps):
                back_stat[step, way] = jnp.where(kind < 8, DEAD, 0.0)

    order = lax.broadcasted_iota(jnp.int32, (8, FREQ // 2), 1).astype(jnp.float32)
    rates = jnp.exp(-jnp.log(jnp.full_like(order, 10000.0)) * order / (FREQ // 2))
    angle = timestep[0].astype(jnp.float32) * rates
    feature = jnp.concatenate([jnp.cos(angle), jnp.sin(angle)], axis=1)
    feature = (feature / (1.0 + jnp.exp(-feature))).astype(jnp.bfloat16)
    polarity = 2.0 * net.astype(jnp.float32) - 1.0
    for copy in own_copies:
        copy.wait()
    for there, block, place in edges:

        @pl.when(jnp.logical_not(there))
        def _():
            for copy in edge_copies(block, place):
                copy.wait()

    @pl.loop(0, heads)
    def _(head):
        at = pl.ds(pl.multiple_of(head * HD, HD), HD)
        gate[:, at] = polarity * jnp.dot(
            feature, proj[:, at], preferred_element_type=jnp.float32
        )

    columns[...] = jnp.zeros_like(columns)
    receive_all(bias_copies())
    for group in range(3):
        for row in range(2):
            bias[2 * group + row] = jnp.broadcast_to(
                bias_in[group, row : row + 1, :], bias.shape[1:]
            )

    @pl.loop(0, steps)
    def _(step):
        receive_all(streams(step))
        start = lanes(step).start
        for j in range(chunk):
            at = pl.ds(pl.multiple_of(start + j * HD, HD), HD)
            q = queries[:, :, at].reshape(6 * block_len, HD)
            k = keys[:, :, at].reshape(4 * block_len, HD)
            v = values[:, :, at].reshape(4 * block_len, HD)
            scores = lax.dot_general(
                q, k, (((1,), (1,)), ((), ())), preferred_element_type=jnp.float32
            )
            scores = scores.reshape(6, block_len // 8, 8, 4 * block_len) + bias[...][:, None]
            scores = scores.reshape(6 * block_len, 4 * block_len)
            top = jnp.max(scores, axis=-1, keepdims=True)
            expo = jnp.exp2((scores - top) * RATE)
            total = jnp.sum(expo, axis=-1, keepdims=True)
            mix = jnp.dot(expo.astype(jnp.bfloat16), v, preferred_element_type=jnp.float32)
            for way in range(2):
                far = slice(2 * way * rows, (2 * way + 1) * rows)
                far_mix[way, :, at] = mix[far].astype(jnp.bfloat16)
                columns[way, :, j : j + 1] = top[far]
                columns[way, :, 8 + j : 9 + j] = total[far]
            own_mix[:, at] = mix[rows : 2 * rows]
            own_top[step, j] = top[rows : 2 * rows]
            own_sum[step, j] = total[rows : 2 * rows]
        for way in range(2):
            far_stat[step, way] = columns[way].T[:16]
        start_all(returns(step))

    def combine(step):
        receive_all(returns(step))
        start = lanes(step).start
        stat = back_stat[step].reshape(32, rows)
        stat = jnp.concatenate([stat, jnp.zeros((HD - 32, rows), jnp.float32)], axis=0).T

        def term(j):
            at = pl.ds(pl.multiple_of(start + j * HD, HD), HD)
            tops = [own_top[step, j], stat[:, j : j + 1], stat[:, 16 + j : 17 + j]]
            sums = [own_sum[step, j], stat[:, 8 + j : 9 + j], stat[:, 24 + j : 25 + j]]
            mixes = [own_mix[:, at]] + [back_mix[way, :, at].astype(jnp.float32) for way in (0, 1)]
            top = jnp.maximum(jnp.maximum(tops[0], tops[1]), tops[2])
            scales = [jnp.exp2((t - top) * RATE) for t in tops]
            whole = 1.0 / sum(a * b for a, b in zip(scales, sums))
            mixed = sum(a * (b * whole) for a, b in zip(mixes, scales))
            return (mixed.reshape(rows // 8, 8, HD) * gate[:, at][None]).reshape(rows, HD)

        @pl.when(step < half)
        def _():
            for j in range(chunk):
                at = pl.ds(pl.multiple_of(step * width + j * HD, HD), HD)
                net_out[:, at] = term(j).astype(jnp.bfloat16)
            crossing(step).start()

        @pl.when(step >= half)
        def _():
            crossing(step - half).wait_recv()
            for j in range(chunk):
                at = pl.ds(pl.multiple_of((step - half) * width + j * HD, HD), HD)
                full = term(j) + net_in[:, at].astype(jnp.float32)
                out[0, :, :, at] = full.astype(jnp.bfloat16).reshape(2, block_len, HD)

    pl.loop(0, steps)(combine)

    sent_all(bias_copies())

    @pl.loop(0, steps)
    def _(step):
        sent_all(streams(step))
        sent_all(returns(step))

    @pl.loop(0, half)
    def _(step):
        crossing(step).wait_send()


def shards(query_rows, key_rows, value_rows, time_proj, block_list, block_count, timestep, *, chunk):
    block_len, features = query_rows.shape[-2:]
    heads = features // HD
    steps = heads // chunk
    rows = 2 * block_len
    bf16, f32 = jnp.bfloat16, jnp.float32
    vmem, dma = pltpu.VMEM, pltpu.SemaphoreType.DMA
    hbm = pl.BlockSpec(memory_space=pltpu.HBM)
    arrays = (query_rows, key_rows, value_rows, time_proj)

    def stay(array):
        return pltpu.with_memory_space_constraint(array, pltpu.HBM)

    pairs = [dma((steps, 2))] * 2
    return pl.pallas_call(
        functools.partial(kernel, chunk),
        out_shape=jax.ShapeDtypeStruct((1, 2, block_len, features // 2), bf16),
        in_specs=[hbm] * 7,
        out_specs=pl.BlockSpec(memory_space=pltpu.VMEM),
        scratch_shapes=[
            pltpu.SMEM(block_list.shape, jnp.int32),
            pltpu.SMEM(block_count.shape, jnp.int32),
            pltpu.SMEM(timestep.shape, jnp.int32),
            vmem((6, block_len, features), bf16),
            vmem((4, block_len, features), bf16),
            vmem((4, block_len, features), bf16),
            vmem((FREQ, features), bf16),
            vmem((8, features), f32),
            vmem((6, 8, 4 * block_len), f32),
            vmem((3, 8, 4 * block_len), f32),
            vmem((2, 8, 4 * block_len), f32),
            vmem((rows, features), f32),
            vmem((steps, chunk, rows, 1), f32),
            vmem((steps, chunk, rows, 1), f32),
            vmem((2, rows, HD), f32),
            vmem((2, rows, features), bf16),
            vmem((steps, 2, 16, rows), f32),
            vmem((2, rows, features), bf16),
            vmem((steps, 2, 16, rows), f32),
            vmem((rows, features // 2), bf16),
            vmem((rows, features // 2), bf16),
            dma((11,)),
            *([dma((2,))] * 2),
            *pairs,
            *pairs,
            *pairs,
            *pairs,
            *pairs,
            *([dma((steps // 2,))] * 2),
        ],
        compiler_params=pltpu.CompilerParams(
            collective_id=0, has_side_effects=True, vmem_limit_bytes=32 << 20
        ),
        name="radial_attention",
    )(stay(block_list), stay(block_count), timestep, *map(stay, arrays))


def solution(mesh, chunk=5):
    return jax.shard_map(
        functools.partial(shards, chunk=chunk),
        mesh=mesh,
        in_specs=(
            P("net", "tm", "space", None, None),
            P("net", "tm", "space", None, None),
            P("net", "tm", "space", None, None),
            P("net", None, None),
            P("tm", "space", None),
            P("tm", "space"),
            P(),
        ),
        out_specs=P("tm", "space", None, "net"),
        check_vma=False,
    )
```

```python
import functools
import math

import jax
import jax.numpy as jnp
from jax import lax
from jax.experimental import pallas as pl
from jax.experimental.pallas import tpu as pltpu
from jax.sharding import PartitionSpec as P

HD = 128
FREQ = 256
DEAD = -1e30
RATE = HD**-0.5 * math.log2(math.e)
MESH = pl.DeviceIdType.MESH


def kernel(
    chunk,
    list_in,
    count_in,
    time_in,
    q_in,
    k_in,
    v_in,
    proj_in,
    out,
    block_list,
    block_count,
    timestep,
    queries,
    keys,
    values,
    proj,
    gate,
    bias,
    bias_in,
    bias_out,
    own_mix,
    own_stat,
    columns,
    scales,
    far_mix,
    far_stat,
    back_mix,
    back_stat,
    net_out,
    net_in,
    local_sem,
    bias_send,
    bias_recv,
    q_send,
    q_recv,
    k_send,
    k_recv,
    v_send,
    v_recv,
    mix_send,
    mix_recv,
    stat_send,
    stat_recv,
    net_send,
    net_recv,
):
    block_len, features = q_in.shape[-2:]
    heads = features // HD
    steps = heads // chunk
    half = steps // 2
    width = chunk * HD
    rows = 2 * block_len
    frames, spaces = lax.axis_size("tm"), lax.axis_size("space")
    frame, space, net = lax.axis_index("tm"), lax.axis_index("space"), lax.axis_index("net")
    down, has_down = {"tm": frame - 1}, frame > 0
    up, has_up = {"tm": frame + 1}, frame < frames - 1
    left, has_left = {"space": space - 1}, space > 0
    right, has_right = {"space": space + 1}, space < spaces - 1
    other = {"net": 1 - net}

    barrier = pltpu.get_barrier_semaphore()
    peers = ((down, has_down), (up, has_up), (left, has_left), (right, has_right))
    for peer, there in peers:

        @pl.when(there)
        def _():
            pl.semaphore_signal(barrier, inc=1, device_id=peer, device_id_type=MESH)

    pl.semaphore_signal(barrier, inc=1, device_id=other, device_id_type=MESH)

    tables = [
        pltpu.make_async_copy(list_in, block_list, local_sem.at[8]),
        pltpu.make_async_copy(count_in, block_count, local_sem.at[9]),
        pltpu.make_async_copy(time_in, timestep, local_sem.at[10]),
    ]
    for copy in tables:
        copy.start()
    own_copies = [
        pltpu.make_async_copy(q_in.at[0, 0], queries.at[pl.ds(2, 2)], local_sem.at[0]),
        pltpu.make_async_copy(k_in.at[0, 0], keys.at[pl.ds(1, 2)], local_sem.at[1]),
        pltpu.make_async_copy(v_in.at[0, 0], values.at[pl.ds(1, 2)], local_sem.at[2]),
        pltpu.make_async_copy(proj_in.at[0], proj, local_sem.at[3]),
    ]
    for copy in own_copies:
        copy.start()

    for copy in tables:
        copy.wait()

    column = lax.broadcasted_iota(jnp.int32, (8, 4 * block_len), 1) // block_len
    sublane = lax.broadcasted_iota(jnp.int32, (8, 4 * block_len), 0)
    slots = block_list.shape[-1]

    def listed(row, frame_step, block_step):
        wanted = (frame + frame_step) * (2 * spaces) + 2 * space + row + block_step
        found = jnp.int32(0)
        for slot in range(slots):
            hit = (block_list[0, row, slot] == wanted) & (slot < block_count[0, row])
            found = found | hit.astype(jnp.int32)
        return jnp.where(found > 0, jnp.float32(0.0), jnp.float32(DEAD))

    def bias_rows(frame_step):
        both = []
        for row in range(2):
            entries = jnp.full(column.shape, DEAD, jnp.float32)
            for place in range(row, row + 3):
                entry = listed(row, frame_step, place - 1 - row)
                entries = jnp.where(column == place, entry, entries)
            both.append(entries)
        return jnp.where(sublane == 0, both[0], both[1])

    bias_out[0] = bias_rows(-1)
    bias_out[1] = bias_rows(1)
    bias_in[1] = bias_rows(0)

    pl.semaphore_wait(barrier, 1 + sum(there.astype(jnp.int32) for _, there in peers))

    def send(src, dst, send_sem, recv_sem, peer):
        return pltpu.make_async_remote_copy(
            src_ref=src,
            dst_ref=dst,
            send_sem=send_sem,
            recv_sem=recv_sem,
            device_id=peer,
            device_id_type=MESH,
        )

    def lanes(step):
        first = lax.rem((1 - net) * (heads // 2) + step * chunk, heads)
        return pl.ds(pl.multiple_of(first * HD, HD), width)

    def half_lanes(step):
        return pl.ds(pl.multiple_of(step * width, HD), width)

    over_z = ((0, down, 2, has_down, has_up), (1, up, 0, has_up, has_down))
    over_space = ((0, left, 3, has_left, has_right), (1, right, 0, has_right, has_left))

    def bias_copies():
        return [
            (
                send(
                    bias_out.at[way], bias_in.at[group], bias_send.at[way], bias_recv.at[way], peer
                ),
                sends,
                receives,
            )
            for way, peer, group, sends, receives in over_z
        ]

    def streams(step):
        at = lanes(step)
        copies = []
        for way, peer, group, sends, receives in over_z:
            copy = send(
                q_in.at[0, 0, :, :, at],
                queries.at[pl.ds(2 * group, 2), :, at],
                q_send.at[step, way],
                q_recv.at[step, way],
                peer,
            )
            copies.append((copy, sends, receives))
        for source, kept, send_sem, recv_sem in (
            (k_in, keys, k_send, k_recv),
            (v_in, values, v_send, v_recv),
        ):
            for way, peer, place, sends, receives in over_space:
                copy = send(
                    source.at[0, 0, way, :, at],
                    kept.at[place, :, at],
                    send_sem.at[step, way],
                    recv_sem.at[step, way],
                    peer,
                )
                copies.append((copy, sends, receives))
        return copies

    def stat_returns(step):
        return [
            (
                send(
                    far_stat.at[step, way],
                    back_stat.at[step, 1 - way],
                    stat_send.at[step, way],
                    stat_recv.at[step, way],
                    peer,
                ),
                sends,
                receives,
            )
            for way, peer, _, sends, receives in over_z
        ]

    def mix_returns(step):
        at = lanes(step)
        return [
            (
                send(
                    far_mix.at[way, :, at],
                    back_mix.at[1 - way, :, at],
                    mix_send.at[step, way],
                    mix_recv.at[step, way],
                    peer,
                ),
                sends,
                receives,
            )
            for way, peer, _, sends, receives in over_z
        ]

    def crossing(step):
        at = half_lanes(step)
        return send(
            net_out.at[:, at], net_in.at[:, at], net_send.at[step], net_recv.at[step], other
        )

    def start_all(copies):
        for copy, sends, _ in copies:
            pl.when(sends)(copy.start)

    def receive_all(copies):
        for copy, _, receives in copies:
            pl.when(receives)(copy.wait_recv)

    def sent_all(copies):
        for copy, sends, _ in copies:
            pl.when(sends)(copy.wait_send)

    start_all(bias_copies())

    @pl.loop(0, steps)
    def _(step):
        start_all(streams(step))

    def edge_copies(block, place):
        return [
            pltpu.make_async_copy(k_in.at[0, 0, block], keys.at[place], local_sem.at[4 + block]),
            pltpu.make_async_copy(v_in.at[0, 0, block], values.at[place], local_sem.at[6 + block]),
        ]

    edges = ((has_left, 0, 0), (has_right, 1, 3))
    for there, block, place in edges:

        @pl.when(jnp.logical_not(there))
        def _():
            for copy in edge_copies(block, place):
                copy.start()

    for there, way in ((has_down, 0), (has_up, 1)):

        @pl.when(jnp.logical_not(there))
        def _():
            for block in range(2):
                queries[4 * way + block] = jnp.zeros((block_len, features), queries.dtype)
            bias_in[2 * way] = jnp.full(bias_in.shape[1:], DEAD, jnp.float32)
            back_mix[way] = jnp.zeros(back_mix.shape[1:], back_mix.dtype)
            kind = lax.broadcasted_iota(jnp.int32, back_stat.shape[2:], 0)
            for step in range(steps):
                back_stat[step, way] = jnp.where(kind < 8, DEAD, 0.0)

    order = lax.broadcasted_iota(jnp.int32, (8, FREQ // 2), 1).astype(jnp.float32)
    rates = jnp.exp(-jnp.log(jnp.full_like(order, 10000.0)) * order / (FREQ // 2))
    angle = timestep[0].astype(jnp.float32) * rates
    feature = jnp.concatenate([jnp.cos(angle), jnp.sin(angle)], axis=1)
    feature = (feature / (1.0 + jnp.exp(-feature))).astype(jnp.bfloat16)
    polarity = 2.0 * net.astype(jnp.float32) - 1.0
    for copy in own_copies:
        copy.wait()
    for there, block, place in edges:

        @pl.when(jnp.logical_not(there))
        def _():
            for copy in edge_copies(block, place):
                copy.wait()

    @pl.loop(0, heads)
    def _(head):
        at = pl.ds(pl.multiple_of(head * HD, HD), HD)
        gate[:, at] = polarity * jnp.dot(
            feature, proj[:, at], preferred_element_type=jnp.float32
        )

    columns[...] = jnp.zeros_like(columns)
    receive_all(bias_copies())
    for group in range(3):
        for row in range(2):
            bias[2 * group + row] = jnp.broadcast_to(
                bias_in[group, row : row + 1, :], bias.shape[1:]
            )

    @pl.loop(0, steps)
    def _(step):
        receive_all(streams(step))
        start = lanes(step).start
        for j in range(chunk):
            at = pl.ds(pl.multiple_of(start + j * HD, HD), HD)
            q = queries[:, :, at].reshape(6 * block_len, HD)
            k = keys[:, :, at].reshape(4 * block_len, HD)
            v = values[:, :, at].reshape(4 * block_len, HD)
            scores = lax.dot_general(
                q, k, (((1,), (1,)), ((), ())), preferred_element_type=jnp.float32
            )
            scores = scores.reshape(6, block_len // 8, 8, 4 * block_len) + bias[...][:, None]
            scores = scores.reshape(6 * block_len, 4 * block_len)
            top = jnp.max(scores, axis=-1, keepdims=True)
            expo = jnp.exp2((scores - top) * RATE)
            total = jnp.sum(expo, axis=-1, keepdims=True)
            mix = jnp.dot(expo.astype(jnp.bfloat16), v, preferred_element_type=jnp.float32)
            for group in range(3):
                part = slice(group * rows, (group + 1) * rows)
                columns[group, :, j : j + 1] = top[part]
                columns[group, :, 8 + j : 9 + j] = total[part]
            far_mix[0, :, at] = mix[:rows].astype(jnp.bfloat16)
            own_mix[:, at] = mix[rows : 2 * rows]
            far_mix[1, :, at] = mix[2 * rows :].astype(jnp.bfloat16)
        far_stat[step, 0] = columns[0].T[:16]
        own_stat[step] = columns[1].T[:16]
        far_stat[step, 1] = columns[2].T[:16]
        start_all(stat_returns(step))
        start_all(mix_returns(step))

    def combine(step):
        start = lanes(step).start
        receive_all(stat_returns(step))
        stats = [own_stat[step], back_stat[step, 0], back_stat[step, 1]]
        top = functools.reduce(jnp.maximum, [stat[:8] for stat in stats])
        shares = [jnp.exp2((stat[:8] - top) * RATE) for stat in stats]
        whole = 1.0 / sum(share * stat[8:] for share, stat in zip(shares, stats))
        shares = [share * whole for share in shares]
        shares = jnp.concatenate([*shares, jnp.zeros((HD - 24, rows), jnp.float32)], axis=0).T

        def head_lanes(j):
            return pl.ds(pl.multiple_of(start + j * HD, HD), HD)

        for j in range(chunk):
            at = head_lanes(j)
            gates = jnp.broadcast_to(gate[:1, at], (rows, HD))
            own_mix[:, at] = own_mix[:, at] * (shares[:, j : j + 1] * gates)
            for way in range(2):
                column = 8 + 8 * way + j
                scales[way, j] = shares[:, column : column + 1] * gates

        def term(j):
            at = head_lanes(j)
            parts = [scales[way, j] * back_mix[way, :, at].astype(jnp.float32) for way in (0, 1)]
            return own_mix[:, at] + parts[0] + parts[1]

        @pl.when(step < half)
        def _():
            receive_all(mix_returns(step))
            for j in range(chunk):
                at = pl.ds(pl.multiple_of(step * width + j * HD, HD), HD)
                net_out[:, at] = term(j).astype(jnp.bfloat16)
            crossing(step).start()

        @pl.when(step >= half)
        def _():
            crossing(step - half).wait_recv()
            receive_all(mix_returns(step))
            for j in range(chunk):
                at = pl.ds(pl.multiple_of((step - half) * width + j * HD, HD), HD)
                full = term(j) + net_in[:, at].astype(jnp.float32)
                out[0, :, :, at] = full.astype(jnp.bfloat16).reshape(2, block_len, HD)

    pl.loop(0, steps)(combine)

    sent_all(bias_copies())

    @pl.loop(0, steps)
    def _(step):
        sent_all(streams(step))
        sent_all(stat_returns(step))
        sent_all(mix_returns(step))

    @pl.loop(0, half)
    def _(step):
        crossing(step).wait_send()


def shards(query_rows, key_rows, value_rows, time_proj, block_list, block_count, timestep, *, chunk):
    block_len, features = query_rows.shape[-2:]
    heads = features // HD
    steps = heads // chunk
    rows = 2 * block_len
    bf16, f32 = jnp.bfloat16, jnp.float32
    vmem, dma = pltpu.VMEM, pltpu.SemaphoreType.DMA
    hbm = pl.BlockSpec(memory_space=pltpu.HBM)
    arrays = (query_rows, key_rows, value_rows, time_proj)

    def stay(array):
        return pltpu.with_memory_space_constraint(array, pltpu.HBM)

    pairs = [dma((steps, 2))] * 2
    return pl.pallas_call(
        functools.partial(kernel, chunk),
        out_shape=jax.ShapeDtypeStruct((1, 2, block_len, features // 2), bf16),
        in_specs=[hbm] * 7,
        out_specs=pl.BlockSpec(memory_space=pltpu.VMEM),
        scratch_shapes=[
            pltpu.SMEM(block_list.shape, jnp.int32),
            pltpu.SMEM(block_count.shape, jnp.int32),
            pltpu.SMEM(timestep.shape, jnp.int32),
            vmem((6, block_len, features), bf16),
            vmem((4, block_len, features), bf16),
            vmem((4, block_len, features), bf16),
            vmem((FREQ, features), bf16),
            vmem((8, features), f32),
            vmem((6, 8, 4 * block_len), f32),
            vmem((3, 8, 4 * block_len), f32),
            vmem((2, 8, 4 * block_len), f32),
            vmem((rows, features), f32),
            vmem((steps, 16, rows), f32),
            vmem((3, rows, HD), f32),
            vmem((2, chunk, rows, HD), f32),
            vmem((2, rows, features), bf16),
            vmem((steps, 2, 16, rows), f32),
            vmem((2, rows, features), bf16),
            vmem((steps, 2, 16, rows), f32),
            vmem((rows, features // 2), bf16),
            vmem((rows, features // 2), bf16),
            dma((11,)),
            *([dma((2,))] * 2),
            *pairs,
            *pairs,
            *pairs,
            *pairs,
            *pairs,
            *([dma((steps // 2,))] * 2),
        ],
        compiler_params=pltpu.CompilerParams(
            collective_id=0, has_side_effects=True, vmem_limit_bytes=32 << 20
        ),
        name="radial_attention",
    )(stay(block_list), stay(block_count), timestep, *map(stay, arrays))


def solution(mesh, chunk=5):
    return jax.shard_map(
        functools.partial(shards, chunk=chunk),
        mesh=mesh,
        in_specs=(
            P("net", "tm", "space", None, None),
            P("net", "tm", "space", None, None),
            P("net", "tm", "space", None, None),
            P("net", None, None),
            P("tm", "space", None),
            P("tm", "space"),
            P(),
        ),
        out_specs=P("tm", "space", None, "net"),
        check_vma=False,
    )
```

```python
import functools
import math

import jax
import jax.numpy as jnp
from jax import lax
from jax.experimental import pallas as pl
from jax.experimental.pallas import tpu as pltpu
from jax.sharding import PartitionSpec as P

HD = 128
FREQ = 256
DEAD = -1e30
RATE = HD**-0.5 * math.log2(math.e)
MESH = pl.DeviceIdType.MESH
AHEAD = 3


def kernel(
    chunk,
    list_in,
    count_in,
    time_in,
    q_in,
    k_in,
    v_in,
    proj_in,
    out,
    block_list,
    block_count,
    timestep,
    queries,
    keys,
    values,
    proj,
    gate,
    bias,
    bias_in,
    bias_out,
    own_mix,
    own_stat,
    columns,
    scales,
    far_mix,
    far_stat,
    back_mix,
    back_stat,
    few_mix,
    share_out,
    share_in,
    pair_out,
    pair_in,
    both_out,
    both_in,
    net_out,
    net_in,
    local_sem,
    bias_send,
    bias_recv,
    q_send,
    q_recv,
    k_send,
    k_recv,
    v_send,
    v_recv,
    mix_send,
    mix_recv,
    stat_send,
    stat_recv,
    share_send,
    share_recv,
    pair_send,
    pair_recv,
    both_send,
    both_recv,
    net_send,
    net_recv,
):
    block_len, features = q_in.shape[-2:]
    heads = features // HD
    kept = heads // 2
    few = chunk // 2
    half = (kept - few) // chunk
    steps = 1 + 2 * half
    width = chunk * HD
    rows = 2 * block_len
    frames, spaces = lax.axis_size("tm"), lax.axis_size("space")
    frame, space, net = lax.axis_index("tm"), lax.axis_index("space"), lax.axis_index("net")
    down, has_down = {"tm": frame - 1}, frame > 0
    up, has_up = {"tm": frame + 1}, frame < frames - 1
    left, has_left = {"space": space - 1}, space > 0
    right, has_right = {"space": space + 1}, space < spaces - 1
    other = {"net": 1 - net}

    barrier = pltpu.get_barrier_semaphore()
    peers = ((down, has_down), (up, has_up), (left, has_left), (right, has_right))
    for peer, there in peers:

        @pl.when(there)
        def _():
            pl.semaphore_signal(barrier, inc=1, device_id=peer, device_id_type=MESH)

    pl.semaphore_signal(barrier, inc=1, device_id=other, device_id_type=MESH)

    tables = [
        pltpu.make_async_copy(list_in, block_list, local_sem.at[8]),
        pltpu.make_async_copy(count_in, block_count, local_sem.at[9]),
        pltpu.make_async_copy(time_in, timestep, local_sem.at[10]),
    ]
    for copy in tables:
        copy.start()
    own_copies = [
        pltpu.make_async_copy(q_in.at[0, 0], queries.at[pl.ds(2, 2)], local_sem.at[0]),
        pltpu.make_async_copy(k_in.at[0, 0], keys.at[pl.ds(1, 2)], local_sem.at[1]),
        pltpu.make_async_copy(v_in.at[0, 0], values.at[pl.ds(1, 2)], local_sem.at[2]),
        pltpu.make_async_copy(proj_in.at[0], proj, local_sem.at[3]),
    ]
    for copy in own_copies:
        copy.start()

    for copy in tables:
        copy.wait()

    column = lax.broadcasted_iota(jnp.int32, (8, 4 * block_len), 1) // block_len
    sublane = lax.broadcasted_iota(jnp.int32, (8, 4 * block_len), 0)
    slots = block_list.shape[-1]

    def listed(row, frame_step, block_step):
        wanted = (frame + frame_step) * (2 * spaces) + 2 * space + row + block_step
        found = jnp.int32(0)
        for slot in range(slots):
            hit = (block_list[0, row, slot] == wanted) & (slot < block_count[0, row])
            found = found | hit.astype(jnp.int32)
        return jnp.where(found > 0, jnp.float32(0.0), jnp.float32(DEAD))

    def bias_rows(frame_step):
        both = []
        for row in range(2):
            entries = jnp.full(column.shape, DEAD, jnp.float32)
            for place in range(row, row + 3):
                entry = listed(row, frame_step, place - 1 - row)
                entries = jnp.where(column == place, entry, entries)
            both.append(entries)
        return jnp.where(sublane == 0, both[0], both[1])

    bias_out[0] = bias_rows(-1)
    bias_out[1] = bias_rows(1)
    bias_in[1] = bias_rows(0)

    pl.semaphore_wait(barrier, 1 + sum(there.astype(jnp.int32) for _, there in peers))

    def send(src, dst, send_sem, recv_sem, peer):
        return pltpu.make_async_remote_copy(
            src_ref=src,
            dst_ref=dst,
            send_sem=send_sem,
            recv_sem=recv_sem,
            device_id=peer,
            device_id_type=MESH,
        )

    theirs, ours = (1 - net) * kept * HD, net * kept * HD

    def offset_of(step):
        return few * HD + lax.rem(step - 1, half) * width

    def first_lane(step):
        return jnp.where(step <= half, theirs, ours) + offset_of(step)

    def pieces(step):
        if isinstance(step, int) and step == 0:
            return [
                (number, pl.ds(pl.multiple_of(start, HD), few * HD))
                for number, start in ((0, theirs), (steps, ours))
            ]
        return [(step, pl.ds(pl.multiple_of(first_lane(step), HD), width))]

    def head_lanes(step, j):
        if isinstance(step, int) and step == 0:
            start = theirs + j * HD if j < few else ours + (j - few) * HD
        else:
            start = first_lane(step) + j * HD
        return pl.ds(pl.multiple_of(start, HD), HD)

    def half_lanes(step, j=None):
        if isinstance(step, int) and step == 0:
            return pl.ds(0, few * HD) if j is None else pl.ds(j * HD, HD)
        if j is None:
            return pl.ds(pl.multiple_of(offset_of(step), HD), width)
        return pl.ds(pl.multiple_of(offset_of(step) + j * HD, HD), HD)

    over_z = ((0, down, 2, has_down, has_up), (1, up, 0, has_up, has_down))
    over_space = ((0, left, 3, has_left, has_right), (1, right, 0, has_right, has_left))

    def bias_copies():
        return [
            (
                send(
                    bias_out.at[way], bias_in.at[group], bias_send.at[way], bias_recv.at[way], peer
                ),
                sends,
                receives,
            )
            for way, peer, group, sends, receives in over_z
        ]

    def query_copies(step):
        return [
            (
                send(
                    q_in.at[0, 0, :, :, at],
                    queries.at[pl.ds(2 * group, 2), :, at],
                    q_send.at[number, way],
                    q_recv.at[number, way],
                    peer,
                ),
                sends,
                receives,
            )
            for number, at in pieces(step)
            for way, peer, group, sends, receives in over_z
        ]

    def key_copies(step):
        return [
            (
                send(
                    source.at[0, 0, way, :, at],
                    held.at[slot, :, at],
                    send_sem.at[number, way],
                    recv_sem.at[number, way],
                    peer,
                ),
                sends,
                receives,
            )
            for number, at in pieces(step)
            for source, held, send_sem, recv_sem in (
                (k_in, keys, k_send, k_recv),
                (v_in, values, v_send, v_recv),
            )
            for way, peer, slot, sends, receives in over_space
        ]

    def returning(far, back, send_sem, recv_sem):
        return [
            (
                send(far.at[way], back.at[1 - way], send_sem.at[way], recv_sem.at[way], peer),
                sends,
                receives,
            )
            for way, peer, _, sends, receives in over_z
        ]

    def share_copies():
        return returning(share_out, share_in, share_send, share_recv)

    def both_copies():
        return returning(both_out, both_in, both_send, both_recv)

    def pair_copy():
        return send(pair_out, pair_in, pair_send.at[0], pair_recv.at[0], other)

    def stat_returns(step):
        return [
            (
                send(
                    far_stat.at[step, way],
                    back_stat.at[step, 1 - way],
                    stat_send.at[step, way],
                    stat_recv.at[step, way],
                    peer,
                ),
                sends,
                receives,
            )
            for way, peer, _, sends, receives in over_z
        ]

    def mix_returns(step):
        [(_, at)] = pieces(step)
        return [
            (
                send(
                    far_mix.at[way, :, at],
                    back_mix.at[1 - way, :, at],
                    mix_send.at[step, way],
                    mix_recv.at[step, way],
                    peer,
                ),
                sends,
                receives,
            )
            for way, peer, _, sends, receives in over_z
        ]

    def crossing(step):
        at = half_lanes(step)
        return send(
            net_out.at[:, at], net_in.at[:, at], net_send.at[step], net_recv.at[step], other
        )

    def start_all(copies):
        for copy, sends, _ in copies:
            pl.when(sends)(copy.start)

    def receive_all(copies):
        for copy, _, receives in copies:
            pl.when(receives)(copy.wait_recv)

    def sent_all(copies):
        for copy, sends, _ in copies:
            pl.when(sends)(copy.wait_send)

    start_all(bias_copies())

    start_all(query_copies(0) + key_copies(0))
    for step in range(1, AHEAD):
        start_all(query_copies(step))

    @pl.loop(1, steps)
    def _(step):
        start_all(key_copies(step))

    def edge_copies(block, place):
        return [
            pltpu.make_async_copy(k_in.at[0, 0, block], keys.at[place], local_sem.at[4 + block]),
            pltpu.make_async_copy(v_in.at[0, 0, block], values.at[place], local_sem.at[6 + block]),
        ]

    edges = ((has_left, 0, 0), (has_right, 1, 3))
    for there, block, place in edges:

        @pl.when(jnp.logical_not(there))
        def _():
            for copy in edge_copies(block, place):
                copy.start()

    for there, way in ((has_down, 0), (has_up, 1)):

        @pl.when(jnp.logical_not(there))
        def _():
            for block in range(2):
                queries[4 * way + block] = jnp.zeros((block_len, features), queries.dtype)
            bias_in[2 * way] = jnp.full(bias_in.shape[1:], DEAD, jnp.float32)
            back_mix[way] = jnp.zeros(back_mix.shape[1:], back_mix.dtype)
            kind = lax.broadcasted_iota(jnp.int32, back_stat.shape[2:], 0)
            for step in range(steps):
                back_stat[step, way] = jnp.where(kind < 4, DEAD, 0.0)
            share_in[way] = jnp.zeros(share_in.shape[1:], jnp.float32)
            both_in[way] = jnp.zeros(both_in.shape[1:], both_in.dtype)

    order = lax.broadcasted_iota(jnp.int32, (8, FREQ // 2), 1).astype(jnp.float32)
    rates = jnp.exp(-jnp.log(jnp.full_like(order, 10000.0)) * order / (FREQ // 2))
    angle = timestep[0].astype(jnp.float32) * rates
    feature = jnp.concatenate([jnp.cos(angle), jnp.sin(angle)], axis=1)
    feature = (feature / (1.0 + jnp.exp(-feature))).astype(jnp.bfloat16)
    polarity = 2.0 * net.astype(jnp.float32) - 1.0
    for copy in own_copies:
        copy.wait()
    for there, block, place in edges:

        @pl.when(jnp.logical_not(there))
        def _():
            for copy in edge_copies(block, place):
                copy.wait()

    @pl.loop(0, heads)
    def _(head):
        at = pl.ds(pl.multiple_of(head * HD, HD), HD)
        gate[:, at] = polarity * jnp.dot(
            feature, proj[:, at], preferred_element_type=jnp.float32
        )

    columns[...] = jnp.zeros_like(columns)
    receive_all(bias_copies())
    for group in range(3):
        for row in range(2):
            bias[2 * group + row] = jnp.broadcast_to(
                bias_in[group, row : row + 1, :], bias.shape[1:]
            )

    def attend(step):
        receive_all(query_copies(step) + key_copies(step))
        for j in range(chunk):
            at = head_lanes(step, j)
            q = queries[:, :, at].reshape(6 * block_len, HD)
            k = keys[:, :, at].reshape(4 * block_len, HD)
            v = values[:, :, at].reshape(4 * block_len, HD)
            scores = lax.dot_general(
                q, k, (((1,), (1,)), ((), ())), preferred_element_type=jnp.float32
            )
            scores = scores.reshape(6, block_len // 8, 8, 4 * block_len) + bias[...][:, None]
            scores = scores.reshape(6 * block_len, 4 * block_len)
            top = jnp.max(scores, axis=-1, keepdims=True)
            expo = jnp.exp2((scores - top) * RATE)
            total = jnp.sum(expo, axis=-1, keepdims=True)
            mix = jnp.dot(expo.astype(jnp.bfloat16), v, preferred_element_type=jnp.float32)
            for group in range(3):
                part = slice(group * rows, (group + 1) * rows)
                columns[group, :, j : j + 1] = top[part]
                columns[group, :, 4 + j : 5 + j] = total[part]
            own_mix[:, at] = mix[rows : 2 * rows]
            for way, part in ((0, mix[:rows]), (1, mix[2 * rows :])):
                if isinstance(step, int) and step == 0:
                    few_mix[way, :, j * HD : (j + 1) * HD] = part
                else:
                    far_mix[way, :, at] = part.astype(jnp.bfloat16)
        far_stat[step, 0] = columns[0].T[:8]
        own_stat[step] = columns[1].T[:8]
        far_stat[step, 1] = columns[2].T[:8]
        start_all(stat_returns(step))

    def shares_of(step):
        receive_all(stat_returns(step))
        stats = [own_stat[step], back_stat[step, 0], back_stat[step, 1]]
        top = functools.reduce(jnp.maximum, stats)
        shares = [jnp.exp2((stat - top) * RATE) for stat in stats]
        sums = [pltpu.roll(stat, 4, 0) for stat in stats]
        whole = 1.0 / sum(share * total for share, total in zip(shares, sums))
        return [share * whole for share in shares]

    def upright(tiles):
        filler = jnp.zeros((HD - 8 * len(tiles), rows), jnp.float32)
        return jnp.concatenate([*tiles, filler], axis=0).T

    def gates_of(at):
        return jnp.broadcast_to(gate[:1, at], (rows, HD))

    def tell_shares():
        shares = shares_of(0)
        share_out[0] = shares[1]
        share_out[1] = shares[2]
        start_all(share_copies())
        share = upright(shares[:1])
        for j in range(chunk):
            at = head_lanes(0, j)
            own = own_mix[:, at] * (share[:, j : j + 1] * gates_of(at))
            if j < few:
                net_out[:, half_lanes(0, j)] = own.astype(jnp.bfloat16)
            else:
                own_mix[:, at] = own
        crossing(0).start()

    def exchange_halves():
        receive_all(share_copies())
        share = upright([share_in[0], share_in[1]])
        for way in range(2):
            for j in range(chunk):
                column = 8 * way + j
                here = pl.ds(j * HD, HD)
                part = few_mix[way, :, here] * (
                    share[:, column : column + 1] * gates_of(head_lanes(0, j))
                )
                if j < few:
                    pair_out[way, :, here] = part.astype(jnp.bfloat16)
                else:
                    few_mix[way, :, here] = part
        pair_copy().start()

    def return_sums():
        pair_copy().wait_recv()
        for way in range(2):
            both_out[way] = (
                few_mix[way, :, few * HD :] + pair_in[way].astype(jnp.float32)
            ).astype(jnp.bfloat16)
        start_all(both_copies())

    attend(0)

    @pl.loop(1, steps)
    def _(step):
        @pl.when(step + AHEAD - 1 < steps)
        def _():
            start_all(query_copies(step + AHEAD - 1))

        attend(step)
        pl.when(step == 1)(tell_shares)
        start_all(mix_returns(step))
        pl.when(step == 2)(exchange_halves)
        pl.when(step == min(3, steps - 1))(return_sums)

    def combine(step):
        shares = upright(shares_of(step))
        for j in range(chunk):
            at = head_lanes(step, j)
            gates = gates_of(at)
            own_mix[:, at] = own_mix[:, at] * (shares[:, j : j + 1] * gates)
            for way in range(2):
                column = 8 + 8 * way + j
                scales[way, j] = shares[:, column : column + 1] * gates

        def term(j):
            at = head_lanes(step, j)
            parts = [scales[way, j] * back_mix[way, :, at].astype(jnp.float32) for way in (0, 1)]
            return own_mix[:, at] + parts[0] + parts[1]

        @pl.when(step <= half)
        def _():
            receive_all(mix_returns(step))
            for j in range(chunk):
                net_out[:, half_lanes(step, j)] = term(j).astype(jnp.bfloat16)
            crossing(step).start()

        @pl.when(step > half)
        def _():
            crossing(step - half).wait_recv()
            receive_all(mix_returns(step))
            for j in range(chunk):
                at = half_lanes(step, j)
                full = term(j) + net_in[:, at].astype(jnp.float32)
                out[0, :, :, at] = full.astype(jnp.bfloat16).reshape(2, block_len, HD)

    def combine_few():
        crossing(0).wait_recv()
        receive_all(both_copies())
        for j in range(few):
            at = half_lanes(0, j)
            full = own_mix[:, head_lanes(0, few + j)] + net_in[:, at].astype(jnp.float32)
            for way in range(2):
                full = full + both_in[way, :, at].astype(jnp.float32)
            out[0, :, :, at] = full.astype(jnp.bfloat16).reshape(2, block_len, HD)

    pl.loop(1, steps - 1)(combine)
    combine_few()
    combine(steps - 1)

    sent_all(bias_copies())

    sent_all(query_copies(0) + key_copies(0) + stat_returns(0))

    @pl.loop(1, steps)
    def _(step):
        sent_all(query_copies(step) + key_copies(step))
        sent_all(stat_returns(step) + mix_returns(step))

    sent_all(share_copies() + both_copies())
    pair_copy().wait_send()
    for step in range(half + 1):
        crossing(step).wait_send()


def shards(query_rows, key_rows, value_rows, time_proj, block_list, block_count, timestep, *, chunk):
    block_len, features = query_rows.shape[-2:]
    heads = features // HD
    few = chunk // 2
    half = (heads // 2 - few) // chunk
    steps = 1 + 2 * half
    rows = 2 * block_len
    bf16, f32 = jnp.bfloat16, jnp.float32
    vmem, dma = pltpu.VMEM, pltpu.SemaphoreType.DMA
    hbm = pl.BlockSpec(memory_space=pltpu.HBM)
    arrays = (query_rows, key_rows, value_rows, time_proj)

    def stay(array):
        return pltpu.with_memory_space_constraint(array, pltpu.HBM)

    pairs = [dma((steps, 2))] * 2
    pieces = [dma((steps + 1, 2))] * 2
    return pl.pallas_call(
        functools.partial(kernel, chunk),
        out_shape=jax.ShapeDtypeStruct((1, 2, block_len, features // 2), bf16),
        in_specs=[hbm] * 7,
        out_specs=pl.BlockSpec(memory_space=pltpu.VMEM),
        scratch_shapes=[
            pltpu.SMEM(block_list.shape, jnp.int32),
            pltpu.SMEM(block_count.shape, jnp.int32),
            pltpu.SMEM(timestep.shape, jnp.int32),
            vmem((6, block_len, features), bf16),
            vmem((4, block_len, features), bf16),
            vmem((4, block_len, features), bf16),
            vmem((FREQ, features), bf16),
            vmem((8, features), f32),
            vmem((6, 8, 4 * block_len), f32),
            vmem((3, 8, 4 * block_len), f32),
            vmem((2, 8, 4 * block_len), f32),
            vmem((rows, features), f32),
            vmem((steps, 8, rows), f32),
            vmem((3, rows, HD), f32),
            vmem((2, chunk, rows, HD), f32),
            vmem((2, rows, features), bf16),
            vmem((steps, 2, 8, rows), f32),
            vmem((2, rows, features), bf16),
            vmem((steps, 2, 8, rows), f32),
            vmem((2, rows, chunk * HD), f32),
            *([vmem((2, 8, rows), f32)] * 2),
            *([vmem((2, rows, few * HD), bf16)] * 2),
            *([vmem((2, rows, few * HD), bf16)] * 2),
            vmem((rows, features // 2), bf16),
            vmem((rows, features // 2), bf16),
            dma((11,)),
            *([dma((2,))] * 2),
            *pieces,
            *pieces,
            *pieces,
            *pairs,
            *pairs,
            *([dma((2,))] * 2),
            *([dma((1,))] * 2),
            *([dma((2,))] * 2),
            *([dma((half + 1,))] * 2),
        ],
        compiler_params=pltpu.CompilerParams(
            collective_id=0, has_side_effects=True, vmem_limit_bytes=32 << 20
        ),
        name="radial_attention",
    )(stay(block_list), stay(block_count), timestep, *map(stay, arrays))


def solution(mesh, chunk=4):
    return jax.shard_map(
        functools.partial(shards, chunk=chunk),
        mesh=mesh,
        in_specs=(
            P("net", "tm", "space", None, None),
            P("net", "tm", "space", None, None),
            P("net", "tm", "space", None, None),
            P("net", None, None),
            P("tm", "space", None),
            P("tm", "space"),
            P(),
        ),
        out_specs=P("tm", "space", None, "net"),
        check_vma=False,
    )
```

```python
import functools
import math

import jax
import jax.numpy as jnp
from jax import lax
from jax.experimental import pallas as pl
from jax.experimental.pallas import tpu as pltpu
from jax.sharding import PartitionSpec as P

HD = 128
FREQ = 256
DEAD = -1e30
RATE = HD**-0.5 * math.log2(math.e)
MESH = pl.DeviceIdType.MESH
LINES = 4
AHEAD = 3


def kernel(
    chunk,
    list_in,
    count_in,
    time_in,
    q_in,
    k_in,
    v_in,
    proj_in,
    out,
    block_list,
    block_count,
    timestep,
    queries,
    keys,
    values,
    proj,
    gate,
    bias,
    bias_in,
    bias_out,
    own_mix,
    own_stat,
    columns,
    scales,
    far_mix,
    far_stat,
    back_mix,
    back_stat,
    few_mix,
    share_out,
    share_in,
    pair_out,
    pair_in,
    both_out,
    both_in,
    net_out,
    net_in,
    local_sem,
    bias_send,
    bias_recv,
    q_send,
    q_recv,
    k_send,
    k_recv,
    v_send,
    v_recv,
    mix_send,
    mix_recv,
    stat_send,
    stat_recv,
    share_send,
    share_recv,
    pair_send,
    pair_recv,
    both_send,
    both_recv,
    net_send,
    net_recv,
):
    block_len, features = q_in.shape[-2:]
    heads = features // HD
    kept = heads // 2
    few = chunk // 2
    half = (kept - few) // chunk
    steps = 1 + 2 * half
    width = chunk * HD
    rows = 2 * block_len
    frames, spaces = lax.axis_size("tm"), lax.axis_size("space")
    frame, space, net = lax.axis_index("tm"), lax.axis_index("space"), lax.axis_index("net")
    down, has_down = {"tm": frame - 1}, frame > 0
    up, has_up = {"tm": frame + 1}, frame < frames - 1
    left, has_left = {"space": space - 1}, space > 0
    right, has_right = {"space": space + 1}, space < spaces - 1
    other = {"net": 1 - net}

    barrier = pltpu.get_barrier_semaphore()
    peers = ((down, has_down), (up, has_up), (left, has_left), (right, has_right))
    for peer, there in peers:

        @pl.when(there)
        def _():
            pl.semaphore_signal(barrier, inc=1, device_id=peer, device_id_type=MESH)

    pl.semaphore_signal(barrier, inc=1, device_id=other, device_id_type=MESH)

    tables = [
        pltpu.make_async_copy(list_in, block_list, local_sem.at[8]),
        pltpu.make_async_copy(count_in, block_count, local_sem.at[9]),
        pltpu.make_async_copy(time_in, timestep, local_sem.at[10]),
    ]
    for copy in tables:
        copy.start()
    own_copies = [
        pltpu.make_async_copy(q_in.at[0, 0], queries.at[pl.ds(2, 2)], local_sem.at[0]),
        pltpu.make_async_copy(k_in.at[0, 0], keys.at[pl.ds(1, 2)], local_sem.at[1]),
        pltpu.make_async_copy(v_in.at[0, 0], values.at[pl.ds(1, 2)], local_sem.at[2]),
        pltpu.make_async_copy(proj_in.at[0], proj, local_sem.at[3]),
    ]
    for copy in own_copies:
        copy.start()

    for copy in tables:
        copy.wait()

    column = lax.broadcasted_iota(jnp.int32, (2, 4 * block_len), 1) // block_len
    sublane = lax.broadcasted_iota(jnp.int32, (2, 4 * block_len), 0)
    slots = block_list.shape[-1]

    def listed(row, frame_step, block_step):
        wanted = (frame + frame_step) * (2 * spaces) + 2 * space + row + block_step
        found = jnp.int32(0)
        for slot in range(slots):
            hit = (block_list[0, row, slot] == wanted) & (slot < block_count[0, row])
            found = found | hit.astype(jnp.int32)
        return jnp.where(found > 0, jnp.float32(0.0), jnp.float32(DEAD))

    def bias_rows(frame_step):
        both = []
        for row in range(2):
            entries = jnp.full(column.shape, DEAD, jnp.float32)
            for place in range(row, row + 3):
                entry = listed(row, frame_step, place - 1 - row)
                entries = jnp.where(column == place, entry, entries)
            both.append(entries)
        return jnp.where(sublane == 0, both[0], both[1])

    bias_out[0] = bias_rows(-1)
    bias_out[1] = bias_rows(1)
    bias_in[1] = bias_rows(0)

    pl.semaphore_wait(barrier, 1 + sum(there.astype(jnp.int32) for _, there in peers))

    def send(src, dst, send_sem, recv_sem, peer):
        return pltpu.make_async_remote_copy(
            src_ref=src,
            dst_ref=dst,
            send_sem=send_sem,
            recv_sem=recv_sem,
            device_id=peer,
            device_id_type=MESH,
        )

    theirs, ours = (1 - net) * kept * HD, net * kept * HD

    def offset_of(step):
        return few * HD + lax.rem(step - 1, half) * width

    def first_lane(step):
        return jnp.where(step <= half, theirs, ours) + offset_of(step)

    def pieces(step):
        if isinstance(step, int) and step == 0:
            return [
                (number, pl.ds(pl.multiple_of(start, HD), few * HD))
                for number, start in ((0, theirs), (steps, ours))
            ]
        return [(step, pl.ds(pl.multiple_of(first_lane(step), HD), width))]

    def head_lanes(step, j):
        if isinstance(step, int) and step == 0:
            start = theirs + j * HD if j < few else ours + (j - few) * HD
        else:
            start = first_lane(step) + j * HD
        return pl.ds(pl.multiple_of(start, HD), HD)

    def half_lanes(step, j=None):
        if isinstance(step, int) and step == 0:
            return pl.ds(0, few * HD) if j is None else pl.ds(j * HD, HD)
        if j is None:
            return pl.ds(pl.multiple_of(offset_of(step), HD), width)
        return pl.ds(pl.multiple_of(offset_of(step) + j * HD, HD), HD)

    over_z = ((0, down, 2, has_down, has_up), (1, up, 0, has_up, has_down))
    over_space = ((0, left, 3, has_left, has_right), (1, right, 0, has_right, has_left))

    def bias_copies():
        return [
            (
                send(
                    bias_out.at[way], bias_in.at[group], bias_send.at[way], bias_recv.at[way], peer
                ),
                sends,
                receives,
            )
            for way, peer, group, sends, receives in over_z
        ]

    def query_copies(step):
        return [
            (
                send(
                    q_in.at[0, 0, :, :, at],
                    queries.at[pl.ds(2 * group, 2), :, at],
                    q_send.at[number, way],
                    q_recv.at[number, way],
                    peer,
                ),
                sends,
                receives,
            )
            for number, at in pieces(step)
            for way, peer, group, sends, receives in over_z
        ]

    def key_copies(step):
        return [
            (
                send(
                    source.at[0, 0, way, :, at],
                    held.at[slot, :, at],
                    send_sem.at[number, way],
                    recv_sem.at[number, way],
                    peer,
                ),
                sends,
                receives,
            )
            for number, at in pieces(step)
            for source, held, send_sem, recv_sem in (
                (k_in, keys, k_send, k_recv),
                (v_in, values, v_send, v_recv),
            )
            for way, peer, slot, sends, receives in over_space
        ]

    def returning(far, back, send_sem, recv_sem):
        return [
            (
                send(far.at[way], back.at[1 - way], send_sem.at[way], recv_sem.at[way], peer),
                sends,
                receives,
            )
            for way, peer, _, sends, receives in over_z
        ]

    def share_copies():
        return returning(share_out, share_in, share_send, share_recv)

    def both_copies():
        return returning(both_out, both_in, both_send, both_recv)

    def pair_copy():
        return send(pair_out, pair_in, pair_send.at[0], pair_recv.at[0], other)

    def stat_returns(step):
        return [
            (
                send(
                    far_stat.at[step, way],
                    back_stat.at[step, 1 - way],
                    stat_send.at[step, way],
                    stat_recv.at[step, way],
                    peer,
                ),
                sends,
                receives,
            )
            for way, peer, _, sends, receives in over_z
        ]

    def mix_returns(step):
        [(_, at)] = pieces(step)
        return [
            (
                send(
                    far_mix.at[way, :, at],
                    back_mix.at[1 - way, :, at],
                    mix_send.at[step, way],
                    mix_recv.at[step, way],
                    peer,
                ),
                sends,
                receives,
            )
            for way, peer, _, sends, receives in over_z
        ]

    def crossing(step):
        at = half_lanes(step)
        return send(
            net_out.at[:, at], net_in.at[:, at], net_send.at[step], net_recv.at[step], other
        )

    def start_all(copies):
        for copy, sends, _ in copies:
            pl.when(sends)(copy.start)

    def receive_all(copies):
        for copy, _, receives in copies:
            pl.when(receives)(copy.wait_recv)

    def sent_all(copies):
        for copy, sends, _ in copies:
            pl.when(sends)(copy.wait_send)

    start_all(bias_copies())

    start_all(query_copies(0) + key_copies(0))
    for step in range(1, AHEAD):
        start_all(query_copies(step))

    @pl.loop(1, steps)
    def _(step):
        start_all(key_copies(step))

    def edge_copies(block, place):
        return [
            pltpu.make_async_copy(k_in.at[0, 0, block], keys.at[place], local_sem.at[4 + block]),
            pltpu.make_async_copy(v_in.at[0, 0, block], values.at[place], local_sem.at[6 + block]),
        ]

    edges = ((has_left, 0, 0), (has_right, 1, 3))
    for there, block, place in edges:

        @pl.when(jnp.logical_not(there))
        def _():
            for copy in edge_copies(block, place):
                copy.start()

    for there, way in ((has_down, 0), (has_up, 1)):

        @pl.when(jnp.logical_not(there))
        def _():
            for block in range(2):
                queries[4 * way + block] = jnp.zeros((block_len, features), queries.dtype)
            bias_in[2 * way] = jnp.full(bias_in.shape[1:], DEAD, jnp.float32)
            back_mix[way] = jnp.zeros(back_mix.shape[1:], back_mix.dtype)
            for step in range(steps):
                back_stat[step, way] = jnp.full(back_stat.shape[2:], DEAD, jnp.float32)
            share_in[way] = jnp.zeros(share_in.shape[1:], jnp.float32)
            both_in[way] = jnp.zeros(both_in.shape[1:], both_in.dtype)

    order = lax.broadcasted_iota(jnp.int32, (8, FREQ // 2), 1).astype(jnp.float32)
    rates = jnp.exp(-jnp.log(jnp.full_like(order, 10000.0)) * order / (FREQ // 2))
    angle = timestep[0].astype(jnp.float32) * rates
    feature = jnp.concatenate([jnp.cos(angle), jnp.sin(angle)], axis=1)
    feature = (feature / (1.0 + jnp.exp(-feature))).astype(jnp.bfloat16)
    polarity = 2.0 * net.astype(jnp.float32) - 1.0
    for copy in own_copies:
        copy.wait()
    for there, block, place in edges:

        @pl.when(jnp.logical_not(there))
        def _():
            for copy in edge_copies(block, place):
                copy.wait()

    @pl.loop(0, heads)
    def _(head):
        at = pl.ds(pl.multiple_of(head * HD, HD), HD)
        gate[:, at] = polarity * jnp.dot(
            feature, proj[:, at], preferred_element_type=jnp.float32
        )

    columns[...] = jnp.zeros_like(columns)
    receive_all(bias_copies())
    for group in range(3):
        for row in range(2):
            bias[2 * group + row] = jnp.broadcast_to(
                bias_in[group, row : row + 1, :], bias.shape[1:]
            )

    def attend(step):
        receive_all(query_copies(step) + key_copies(step))
        for j in range(chunk):
            at = head_lanes(step, j)
            q = queries[:, :, at].reshape(6 * block_len, HD)
            k = keys[:, :, at].reshape(4 * block_len, HD)
            v = values[:, :, at].reshape(4 * block_len, HD)
            scores = lax.dot_general(
                q, k, (((1,), (1,)), ((), ())), preferred_element_type=jnp.float32
            )
            scores = scores.reshape(6, block_len // 8, 8, 4 * block_len) + bias[...][:, None]
            scores = scores.reshape(6 * block_len, 4 * block_len)
            top = jnp.max(scores, axis=-1, keepdims=True)
            expo = jnp.exp2((scores - top) * RATE)
            total = jnp.sum(expo, axis=-1, keepdims=True)
            weight = top * RATE + jnp.log2(total)
            mix = jnp.dot(expo.astype(jnp.bfloat16), v, preferred_element_type=jnp.float32)
            mix = mix * (1.0 / total)
            for group in range(3):
                part = slice(group * rows, (group + 1) * rows)
                columns[group, :, j : j + 1] = weight[part]
            own_mix[:, at] = mix[rows : 2 * rows]
            for way, part in ((0, mix[:rows]), (1, mix[2 * rows :])):
                if isinstance(step, int) and step == 0:
                    few_mix[way, :, j * HD : (j + 1) * HD] = part
                else:
                    far_mix[way, :, at] = part.astype(jnp.bfloat16)
        far_stat[step, 0] = columns[0].T[:LINES]
        own_stat[step] = columns[1].T[:LINES]
        far_stat[step, 1] = columns[2].T[:LINES]
        start_all(stat_returns(step))

    def shares_of(step):
        receive_all(stat_returns(step))
        weights = [own_stat[step], back_stat[step, 0], back_stat[step, 1]]
        top = functools.reduce(jnp.maximum, weights)
        shares = [jnp.exp2(weight - top) for weight in weights]
        whole = 1.0 / sum(shares)
        return [share * whole for share in shares]

    def upright(tiles):
        filler = jnp.zeros((8 - LINES, rows), jnp.float32)
        tiles = [piece for tile in tiles for piece in (tile, filler)]
        filler = jnp.zeros((HD - 4 * len(tiles), rows), jnp.float32)
        return jnp.concatenate([*tiles, filler], axis=0).T

    def gates_of(at):
        return jnp.broadcast_to(gate[:1, at], (rows, HD))

    def tell_shares():
        shares = shares_of(0)
        share_out[0] = shares[1]
        share_out[1] = shares[2]
        start_all(share_copies())
        share = upright(shares[:1])
        for j in range(chunk):
            at = head_lanes(0, j)
            own = own_mix[:, at] * (share[:, j : j + 1] * gates_of(at))
            if j < few:
                net_out[:, half_lanes(0, j)] = own.astype(jnp.bfloat16)
            else:
                own_mix[:, at] = own
        crossing(0).start()

    def exchange_halves():
        receive_all(share_copies())
        share = upright([share_in[0], share_in[1]])
        for way in range(2):
            for j in range(chunk):
                column = 8 * way + j
                here = pl.ds(j * HD, HD)
                part = few_mix[way, :, here] * (
                    share[:, column : column + 1] * gates_of(head_lanes(0, j))
                )
                if j < few:
                    pair_out[way, :, here] = part.astype(jnp.bfloat16)
                else:
                    few_mix[way, :, here] = part
        pair_copy().start()

    def return_sums():
        pair_copy().wait_recv()
        for way in range(2):
            both_out[way] = (
                few_mix[way, :, few * HD :] + pair_in[way].astype(jnp.float32)
            ).astype(jnp.bfloat16)
        start_all(both_copies())

    attend(0)

    @pl.loop(1, steps)
    def _(step):
        @pl.when(step + AHEAD - 1 < steps)
        def _():
            start_all(query_copies(step + AHEAD - 1))

        attend(step)
        pl.when(step == 1)(tell_shares)
        start_all(mix_returns(step))
        pl.when(step == 2)(exchange_halves)
        pl.when(step == min(3, steps - 1))(return_sums)

    def combine(step):
        shares = upright(shares_of(step))
        for j in range(chunk):
            at = head_lanes(step, j)
            gates = gates_of(at)
            own_mix[:, at] = own_mix[:, at] * (shares[:, j : j + 1] * gates)
            for way in range(2):
                column = 8 + 8 * way + j
                scales[way, j] = shares[:, column : column + 1] * gates

        def term(j):
            at = head_lanes(step, j)
            parts = [scales[way, j] * back_mix[way, :, at].astype(jnp.float32) for way in (0, 1)]
            return own_mix[:, at] + parts[0] + parts[1]

        @pl.when(step <= half)
        def _():
            receive_all(mix_returns(step))
            for j in range(chunk):
                net_out[:, half_lanes(step, j)] = term(j).astype(jnp.bfloat16)
            crossing(step).start()

        @pl.when(step > half)
        def _():
            crossing(step - half).wait_recv()
            receive_all(mix_returns(step))
            for j in range(chunk):
                at = half_lanes(step, j)
                full = term(j) + net_in[:, at].astype(jnp.float32)
                out[0, :, :, at] = full.astype(jnp.bfloat16).reshape(2, block_len, HD)

    def combine_few():
        crossing(0).wait_recv()
        receive_all(both_copies())
        for j in range(few):
            at = half_lanes(0, j)
            full = own_mix[:, head_lanes(0, few + j)] + net_in[:, at].astype(jnp.float32)
            for way in range(2):
                full = full + both_in[way, :, at].astype(jnp.float32)
            out[0, :, :, at] = full.astype(jnp.bfloat16).reshape(2, block_len, HD)

    pl.loop(1, steps - 1)(combine)
    combine_few()

    sent_all(bias_copies() + query_copies(0) + key_copies(0) + stat_returns(0))

    @pl.loop(1, steps)
    def _(step):
        sent_all(query_copies(step) + key_copies(step) + stat_returns(step))

    sent_all(share_copies() + both_copies())
    pair_copy().wait_send()
    for step in range(half + 1):
        crossing(step).wait_send()

    @pl.loop(1, steps - 1)
    def _(step):
        sent_all(mix_returns(step))

    combine(steps - 1)
    sent_all(mix_returns(steps - 1))


def shards(query_rows, key_rows, value_rows, time_proj, block_list, block_count, timestep, *, chunk):
    block_len, features = query_rows.shape[-2:]
    heads = features // HD
    few = chunk // 2
    half = (heads // 2 - few) // chunk
    steps = 1 + 2 * half
    rows = 2 * block_len
    bf16, f32 = jnp.bfloat16, jnp.float32
    vmem, dma = pltpu.VMEM, pltpu.SemaphoreType.DMA
    hbm = pl.BlockSpec(memory_space=pltpu.HBM)
    arrays = (query_rows, key_rows, value_rows, time_proj)

    def stay(array):
        return pltpu.with_memory_space_constraint(array, pltpu.HBM)

    pairs = [dma((steps, 2))] * 2
    pieces = [dma((steps + 1, 2))] * 2
    return pl.pallas_call(
        functools.partial(kernel, chunk),
        out_shape=jax.ShapeDtypeStruct((1, 2, block_len, features // 2), bf16),
        in_specs=[hbm] * 7,
        out_specs=pl.BlockSpec(memory_space=pltpu.VMEM),
        scratch_shapes=[
            pltpu.SMEM(block_list.shape, jnp.int32),
            pltpu.SMEM(block_count.shape, jnp.int32),
            pltpu.SMEM(timestep.shape, jnp.int32),
            vmem((6, block_len, features), bf16),
            vmem((4, block_len, features), bf16),
            vmem((4, block_len, features), bf16),
            vmem((FREQ, features), bf16),
            vmem((8, features), f32),
            vmem((6, 8, 4 * block_len), f32),
            vmem((3, 2, 4 * block_len), f32),
            vmem((2, 2, 4 * block_len), f32),
            vmem((rows, features), f32),
            vmem((steps, LINES, rows), f32),
            vmem((3, rows, HD), f32),
            vmem((2, chunk, rows, HD), f32),
            vmem((2, rows, features), bf16),
            vmem((steps, 2, LINES, rows), f32),
            vmem((2, rows, features), bf16),
            vmem((steps, 2, LINES, rows), f32),
            vmem((2, rows, chunk * HD), f32),
            *([vmem((2, LINES, rows), f32)] * 2),
            *([vmem((2, rows, few * HD), bf16)] * 2),
            *([vmem((2, rows, few * HD), bf16)] * 2),
            vmem((rows, features // 2), bf16),
            vmem((rows, features // 2), bf16),
            dma((11,)),
            *([dma((2,))] * 2),
            *pieces,
            *pieces,
            *pieces,
            *pairs,
            *pairs,
            *([dma((2,))] * 2),
            *([dma((1,))] * 2),
            *([dma((2,))] * 2),
            *([dma((half + 1,))] * 2),
        ],
        compiler_params=pltpu.CompilerParams(
            collective_id=0, has_side_effects=True, vmem_limit_bytes=32 << 20
        ),
        name="radial_attention",
    )(stay(block_list), stay(block_count), timestep, *map(stay, arrays))


def solution(mesh, chunk=4):
    return jax.shard_map(
        functools.partial(shards, chunk=chunk),
        mesh=mesh,
        in_specs=(
            P("net", "tm", "space", None, None),
            P("net", "tm", "space", None, None),
            P("net", "tm", "space", None, None),
            P("net", None, None),
            P("tm", "space", None),
            P("tm", "space"),
            P(),
        ),
        out_specs=P("tm", "space", None, "net"),
        check_vma=False,
    )
```

```python
import functools
import math

import jax
import jax.numpy as jnp
from jax import lax
from jax.experimental import pallas as pl
from jax.experimental.pallas import tpu as pltpu
from jax.sharding import PartitionSpec as P

HD = 128
FREQ = 256
DEAD = -1e30
RATE = HD**-0.5 * math.log2(math.e)
MESH = pl.DeviceIdType.MESH
LINES = 4
AHEAD = 3


def kernel(
    chunk,
    list_in,
    count_in,
    time_in,
    q_in,
    k_in,
    v_in,
    proj_in,
    out,
    block_list,
    block_count,
    timestep,
    queries,
    keys,
    values,
    proj,
    gate,
    bias,
    bias_in,
    bias_out,
    own_mix,
    own_stat,
    columns,
    scales,
    far_mix,
    far_stat,
    back_mix,
    back_stat,
    few_mix,
    share_out,
    share_in,
    pair_out,
    pair_in,
    both_out,
    both_in,
    net_out,
    net_in,
    local_sem,
    bias_send,
    bias_recv,
    q_send,
    q_recv,
    k_send,
    k_recv,
    v_send,
    v_recv,
    mix_send,
    mix_recv,
    stat_send,
    stat_recv,
    share_send,
    share_recv,
    pair_send,
    pair_recv,
    both_send,
    both_recv,
    net_send,
    net_recv,
):
    block_len, features = q_in.shape[-2:]
    heads = features // HD
    kept = heads // 2
    few = chunk // 2
    half = (kept - few) // chunk
    steps = 1 + 2 * half
    width = chunk * HD
    rows = 2 * block_len
    frames, spaces = lax.axis_size("tm"), lax.axis_size("space")
    frame, space, net = lax.axis_index("tm"), lax.axis_index("space"), lax.axis_index("net")
    down, has_down = {"tm": frame - 1}, frame > 0
    up, has_up = {"tm": frame + 1}, frame < frames - 1
    left, has_left = {"space": space - 1}, space > 0
    right, has_right = {"space": space + 1}, space < spaces - 1
    other = {"net": 1 - net}

    barrier = pltpu.get_barrier_semaphore()
    peers = ((down, has_down), (up, has_up), (left, has_left), (right, has_right))
    for peer, there in peers:

        @pl.when(there)
        def _():
            pl.semaphore_signal(barrier, inc=1, device_id=peer, device_id_type=MESH)

    pl.semaphore_signal(barrier, inc=1, device_id=other, device_id_type=MESH)

    tables = [
        pltpu.make_async_copy(list_in, block_list, local_sem.at[8]),
        pltpu.make_async_copy(count_in, block_count, local_sem.at[9]),
        pltpu.make_async_copy(time_in, timestep, local_sem.at[10]),
    ]
    for copy in tables:
        copy.start()
    own_copies = [
        pltpu.make_async_copy(q_in.at[0, 0], queries.at[pl.ds(2, 2)], local_sem.at[0]),
        pltpu.make_async_copy(k_in.at[0, 0], keys.at[pl.ds(1, 2)], local_sem.at[1]),
        pltpu.make_async_copy(v_in.at[0, 0], values.at[pl.ds(1, 2)], local_sem.at[2]),
        pltpu.make_async_copy(proj_in.at[0], proj, local_sem.at[3]),
    ]
    for copy in own_copies:
        copy.start()

    for copy in tables:
        copy.wait()

    column = lax.broadcasted_iota(jnp.int32, (2, 4 * block_len), 1) // block_len
    sublane = lax.broadcasted_iota(jnp.int32, (2, 4 * block_len), 0)
    slots = block_list.shape[-1]

    def listed(row, frame_step, block_step):
        wanted = (frame + frame_step) * (2 * spaces) + 2 * space + row + block_step
        found = jnp.int32(0)
        for slot in range(slots):
            hit = (block_list[0, row, slot] == wanted) & (slot < block_count[0, row])
            found = found | hit.astype(jnp.int32)
        return jnp.where(found > 0, jnp.float32(0.0), jnp.float32(DEAD))

    def bias_rows(frame_step):
        both = []
        for row in range(2):
            entries = jnp.full(column.shape, DEAD, jnp.float32)
            for place in range(row, row + 3):
                entry = listed(row, frame_step, place - 1 - row)
                entries = jnp.where(column == place, entry, entries)
            both.append(entries)
        return jnp.where(sublane == 0, both[0], both[1])

    bias_out[0] = bias_rows(-1)
    bias_out[1] = bias_rows(1)
    bias_in[1] = bias_rows(0)

    pl.semaphore_wait(barrier, 1 + sum(there.astype(jnp.int32) for _, there in peers))

    def send(src, dst, send_sem, recv_sem, peer):
        return pltpu.make_async_remote_copy(
            src_ref=src,
            dst_ref=dst,
            send_sem=send_sem,
            recv_sem=recv_sem,
            device_id=peer,
            device_id_type=MESH,
        )

    theirs, ours = (1 - net) * kept * HD, net * kept * HD

    def offset_of(step):
        return few * HD + lax.rem(step - 1, half) * width

    def first_lane(step):
        return jnp.where(step <= half, theirs, ours) + offset_of(step)

    def pieces(step):
        if isinstance(step, int) and step == 0:
            return [
                (number, pl.ds(pl.multiple_of(start, HD), few * HD))
                for number, start in ((0, theirs), (steps, ours))
            ]
        return [(step, pl.ds(pl.multiple_of(first_lane(step), HD), width))]

    def head_lanes(step, j):
        if isinstance(step, int) and step == 0:
            start = theirs + j * HD if j < few else ours + (j - few) * HD
        else:
            start = first_lane(step) + j * HD
        return pl.ds(pl.multiple_of(start, HD), HD)

    def half_lanes(step, j=None):
        if isinstance(step, int) and step == 0:
            return pl.ds(0, few * HD) if j is None else pl.ds(j * HD, HD)
        if j is None:
            return pl.ds(pl.multiple_of(offset_of(step), HD), width)
        return pl.ds(pl.multiple_of(offset_of(step) + j * HD, HD), HD)

    over_z = ((0, down, 2, has_down, has_up), (1, up, 0, has_up, has_down))
    over_space = ((0, left, 3, has_left, has_right), (1, right, 0, has_right, has_left))

    def bias_copies():
        return [
            (
                send(
                    bias_out.at[way], bias_in.at[group], bias_send.at[way], bias_recv.at[way], peer
                ),
                sends,
                receives,
            )
            for way, peer, group, sends, receives in over_z
        ]

    def query_copies(step):
        return [
            (
                send(
                    q_in.at[0, 0, :, :, at],
                    queries.at[pl.ds(2 * group, 2), :, at],
                    q_send.at[number, way],
                    q_recv.at[number, way],
                    peer,
                ),
                sends,
                receives,
            )
            for number, at in pieces(step)
            for way, peer, group, sends, receives in over_z
        ]

    def key_copies(step):
        return [
            (
                send(
                    source.at[0, 0, way, :, at],
                    held.at[slot, :, at],
                    send_sem.at[number, way],
                    recv_sem.at[number, way],
                    peer,
                ),
                sends,
                receives,
            )
            for number, at in pieces(step)
            for source, held, send_sem, recv_sem in (
                (k_in, keys, k_send, k_recv),
                (v_in, values, v_send, v_recv),
            )
            for way, peer, slot, sends, receives in over_space
        ]

    def returning(far, back, send_sem, recv_sem):
        return [
            (
                send(far.at[way], back.at[1 - way], send_sem.at[way], recv_sem.at[way], peer),
                sends,
                receives,
            )
            for way, peer, _, sends, receives in over_z
        ]

    def share_copies():
        return returning(share_out, share_in, share_send, share_recv)

    def both_copies():
        return returning(both_out, both_in, both_send, both_recv)

    def pair_copy():
        return send(pair_out, pair_in, pair_send.at[0], pair_recv.at[0], other)

    def stat_returns(step):
        return [
            (
                send(
                    far_stat.at[step, way],
                    back_stat.at[step, 1 - way],
                    stat_send.at[step, way],
                    stat_recv.at[step, way],
                    peer,
                ),
                sends,
                receives,
            )
            for way, peer, _, sends, receives in over_z
        ]

    def mix_returns(step, part=None):
        [(number, at)] = pieces(step)
        if part is not None:
            number = (steps - 1, steps)[part]
            at = pl.ds(pl.multiple_of(first_lane(step) + part * few * HD, HD), few * HD)
        return [
            (
                send(
                    far_mix.at[way, :, at],
                    back_mix.at[1 - way, :, at],
                    mix_send.at[number, way],
                    mix_recv.at[number, way],
                    peer,
                ),
                sends,
                receives,
            )
            for way, peer, _, sends, receives in over_z
        ]

    def crossing(step):
        at = half_lanes(step)
        return send(
            net_out.at[:, at], net_in.at[:, at], net_send.at[step], net_recv.at[step], other
        )

    def start_all(copies):
        for copy, sends, _ in copies:
            pl.when(sends)(copy.start)

    def receive_all(copies):
        for copy, _, receives in copies:
            pl.when(receives)(copy.wait_recv)

    def sent_all(copies):
        for copy, sends, _ in copies:
            pl.when(sends)(copy.wait_send)

    start_all(bias_copies())

    start_all(query_copies(0) + key_copies(0))
    for step in range(1, AHEAD):
        start_all(query_copies(step))

    @pl.loop(1, steps)
    def _(step):
        start_all(key_copies(step))

    def edge_copies(block, place):
        return [
            pltpu.make_async_copy(k_in.at[0, 0, block], keys.at[place], local_sem.at[4 + block]),
            pltpu.make_async_copy(v_in.at[0, 0, block], values.at[place], local_sem.at[6 + block]),
        ]

    edges = ((has_left, 0, 0), (has_right, 1, 3))
    for there, block, place in edges:

        @pl.when(jnp.logical_not(there))
        def _():
            for copy in edge_copies(block, place):
                copy.start()

    for there, way in ((has_down, 0), (has_up, 1)):

        @pl.when(jnp.logical_not(there))
        def _():
            for block in range(2):
                queries[4 * way + block] = jnp.zeros((block_len, features), queries.dtype)
            bias_in[2 * way] = jnp.full(bias_in.shape[1:], DEAD, jnp.float32)
            back_mix[way] = jnp.zeros(back_mix.shape[1:], back_mix.dtype)
            for step in range(steps):
                back_stat[step, way] = jnp.full(back_stat.shape[2:], DEAD, jnp.float32)
            share_in[way] = jnp.zeros(share_in.shape[1:], jnp.float32)
            both_in[way] = jnp.zeros(both_in.shape[1:], both_in.dtype)

    order = lax.broadcasted_iota(jnp.int32, (8, FREQ // 2), 1).astype(jnp.float32)
    rates = jnp.exp(-jnp.log(jnp.full_like(order, 10000.0)) * order / (FREQ // 2))
    angle = timestep[0].astype(jnp.float32) * rates
    feature = jnp.concatenate([jnp.cos(angle), jnp.sin(angle)], axis=1)
    feature = (feature / (1.0 + jnp.exp(-feature))).astype(jnp.bfloat16)
    polarity = 2.0 * net.astype(jnp.float32) - 1.0
    for copy in own_copies:
        copy.wait()
    for there, block, place in edges:

        @pl.when(jnp.logical_not(there))
        def _():
            for copy in edge_copies(block, place):
                copy.wait()

    @pl.loop(0, heads)
    def _(head):
        at = pl.ds(pl.multiple_of(head * HD, HD), HD)
        gate[:, at] = polarity * jnp.dot(
            feature, proj[:, at], preferred_element_type=jnp.float32
        )

    columns[...] = jnp.zeros_like(columns)
    receive_all(bias_copies())
    for group in range(3):
        for row in range(2):
            bias[2 * group + row] = jnp.broadcast_to(
                bias_in[group, row : row + 1, :], bias.shape[1:]
            )

    def attend(step):
        receive_all(query_copies(step) + key_copies(step))
        for j in range(chunk):
            at = head_lanes(step, j)
            q = queries[:, :, at].reshape(6 * block_len, HD)
            k = keys[:, :, at].reshape(4 * block_len, HD)
            v = values[:, :, at].reshape(4 * block_len, HD)
            scores = lax.dot_general(
                q, k, (((1,), (1,)), ((), ())), preferred_element_type=jnp.float32
            )
            scores = scores.reshape(6, block_len // 8, 8, 4 * block_len) + bias[...][:, None]
            scores = scores.reshape(6 * block_len, 4 * block_len)
            top = jnp.max(scores, axis=-1, keepdims=True)
            expo = jnp.exp2((scores - top) * RATE)
            total = jnp.sum(expo, axis=-1, keepdims=True)
            weight = top * RATE + jnp.log2(total)
            mix = jnp.dot(expo.astype(jnp.bfloat16), v, preferred_element_type=jnp.float32)
            mix = mix * (1.0 / total)
            for group in range(3):
                part = slice(group * rows, (group + 1) * rows)
                columns[group, :, j : j + 1] = weight[part]
            own_mix[:, at] = mix[rows : 2 * rows]
            for way, part in ((0, mix[:rows]), (1, mix[2 * rows :])):
                if isinstance(step, int) and step == 0:
                    few_mix[way, :, j * HD : (j + 1) * HD] = part
                else:
                    far_mix[way, :, at] = part.astype(jnp.bfloat16)
        far_stat[step, 0] = columns[0].T[:LINES]
        own_stat[step] = columns[1].T[:LINES]
        far_stat[step, 1] = columns[2].T[:LINES]
        start_all(stat_returns(step))

    def shares_of(step):
        receive_all(stat_returns(step))
        weights = [own_stat[step], back_stat[step, 0], back_stat[step, 1]]
        top = functools.reduce(jnp.maximum, weights)
        shares = [jnp.exp2(weight - top) for weight in weights]
        whole = 1.0 / sum(shares)
        return [share * whole for share in shares]

    def upright(tiles):
        filler = jnp.zeros((8 - LINES, rows), jnp.float32)
        tiles = [piece for tile in tiles for piece in (tile, filler)]
        filler = jnp.zeros((HD - 4 * len(tiles), rows), jnp.float32)
        return jnp.concatenate([*tiles, filler], axis=0).T

    def gates_of(at):
        return jnp.broadcast_to(gate[:1, at], (rows, HD))

    def tell_shares():
        shares = shares_of(0)
        share_out[0] = shares[1]
        share_out[1] = shares[2]
        start_all(share_copies())
        share = upright(shares[:1])
        for j in range(chunk):
            at = head_lanes(0, j)
            own = own_mix[:, at] * (share[:, j : j + 1] * gates_of(at))
            if j < few:
                net_out[:, half_lanes(0, j)] = own.astype(jnp.bfloat16)
            else:
                own_mix[:, at] = own
        crossing(0).start()

    def exchange_halves():
        receive_all(share_copies())
        share = upright([share_in[0], share_in[1]])
        for way in range(2):
            for j in range(chunk):
                column = 8 * way + j
                here = pl.ds(j * HD, HD)
                part = few_mix[way, :, here] * (
                    share[:, column : column + 1] * gates_of(head_lanes(0, j))
                )
                if j < few:
                    pair_out[way, :, here] = part.astype(jnp.bfloat16)
                else:
                    few_mix[way, :, here] = part
        pair_copy().start()

    def return_sums():
        pair_copy().wait_recv()
        for way in range(2):
            both_out[way] = (
                few_mix[way, :, few * HD :] + pair_in[way].astype(jnp.float32)
            ).astype(jnp.bfloat16)
        start_all(both_copies())

    attend(0)

    @pl.loop(1, steps)
    def _(step):
        @pl.when(step + AHEAD - 1 < steps)
        def _():
            start_all(query_copies(step + AHEAD - 1))

        attend(step)
        pl.when(step == 1)(tell_shares)

        @pl.when(step < steps - 1)
        def _():
            start_all(mix_returns(step))

        @pl.when(step == steps - 1)
        def _():
            start_all(mix_returns(steps - 1, 0) + mix_returns(steps - 1, 1))

        pl.when(step == 2)(exchange_halves)
        pl.when(step == min(3, steps - 1))(return_sums)

    def combine(step):
        shares = upright(shares_of(step))
        for j in range(chunk):
            at = head_lanes(step, j)
            gates = gates_of(at)
            own_mix[:, at] = own_mix[:, at] * (shares[:, j : j + 1] * gates)
            for way in range(2):
                column = 8 + 8 * way + j
                scales[way, j] = shares[:, column : column + 1] * gates

        def term(j):
            at = head_lanes(step, j)
            parts = [scales[way, j] * back_mix[way, :, at].astype(jnp.float32) for way in (0, 1)]
            return own_mix[:, at] + parts[0] + parts[1]

        @pl.when(step <= half)
        def _():
            receive_all(mix_returns(step))
            for j in range(chunk):
                net_out[:, half_lanes(step, j)] = term(j).astype(jnp.bfloat16)
            crossing(step).start()

        @pl.when(step > half)
        def _():
            crossing(step - half).wait_recv()
            last = isinstance(step, int) and step == steps - 1
            if not last:
                receive_all(mix_returns(step))
            for j in range(chunk):
                if last and j % few == 0:
                    receive_all(mix_returns(step, j // few))
                at = half_lanes(step, j)
                full = term(j) + net_in[:, at].astype(jnp.float32)
                out[0, :, :, at] = full.astype(jnp.bfloat16).reshape(2, block_len, HD)

    def combine_few():
        crossing(0).wait_recv()
        receive_all(both_copies())
        for j in range(few):
            at = half_lanes(0, j)
            full = own_mix[:, head_lanes(0, few + j)] + net_in[:, at].astype(jnp.float32)
            for way in range(2):
                full = full + both_in[way, :, at].astype(jnp.float32)
            out[0, :, :, at] = full.astype(jnp.bfloat16).reshape(2, block_len, HD)

    pl.loop(1, steps - 1)(combine)
    combine_few()

    sent_all(bias_copies() + query_copies(0) + key_copies(0) + stat_returns(0))

    @pl.loop(1, steps)
    def _(step):
        sent_all(query_copies(step) + key_copies(step) + stat_returns(step))

    sent_all(share_copies() + both_copies())
    pair_copy().wait_send()
    for step in range(half + 1):
        crossing(step).wait_send()

    @pl.loop(1, steps - 1)
    def _(step):
        sent_all(mix_returns(step))

    combine(steps - 1)
    sent_all(mix_returns(steps - 1, 0) + mix_returns(steps - 1, 1))


def shards(query_rows, key_rows, value_rows, time_proj, block_list, block_count, timestep, *, chunk):
    block_len, features = query_rows.shape[-2:]
    heads = features // HD
    few = chunk // 2
    half = (heads // 2 - few) // chunk
    steps = 1 + 2 * half
    rows = 2 * block_len
    bf16, f32 = jnp.bfloat16, jnp.float32
    vmem, dma = pltpu.VMEM, pltpu.SemaphoreType.DMA
    hbm = pl.BlockSpec(memory_space=pltpu.HBM)
    arrays = (query_rows, key_rows, value_rows, time_proj)

    def stay(array):
        return pltpu.with_memory_space_constraint(array, pltpu.HBM)

    pairs = [dma((steps, 2))] * 2
    pieces = [dma((steps + 1, 2))] * 2
    return pl.pallas_call(
        functools.partial(kernel, chunk),
        out_shape=jax.ShapeDtypeStruct((1, 2, block_len, features // 2), bf16),
        in_specs=[hbm] * 7,
        out_specs=pl.BlockSpec(memory_space=pltpu.VMEM),
        scratch_shapes=[
            pltpu.SMEM(block_list.shape, jnp.int32),
            pltpu.SMEM(block_count.shape, jnp.int32),
            pltpu.SMEM(timestep.shape, jnp.int32),
            vmem((6, block_len, features), bf16),
            vmem((4, block_len, features), bf16),
            vmem((4, block_len, features), bf16),
            vmem((FREQ, features), bf16),
            vmem((8, features), f32),
            vmem((6, 8, 4 * block_len), f32),
            vmem((3, 2, 4 * block_len), f32),
            vmem((2, 2, 4 * block_len), f32),
            vmem((rows, features), f32),
            vmem((steps, LINES, rows), f32),
            vmem((3, rows, HD), f32),
            vmem((2, chunk, rows, HD), f32),
            vmem((2, rows, features), bf16),
            vmem((steps, 2, LINES, rows), f32),
            vmem((2, rows, features), bf16),
            vmem((steps, 2, LINES, rows), f32),
            vmem((2, rows, chunk * HD), f32),
            *([vmem((2, LINES, rows), f32)] * 2),
            *([vmem((2, rows, few * HD), bf16)] * 2),
            *([vmem((2, rows, few * HD), bf16)] * 2),
            vmem((rows, features // 2), bf16),
            vmem((rows, features // 2), bf16),
            dma((11,)),
            *([dma((2,))] * 2),
            *pieces,
            *pieces,
            *pieces,
            *pieces,
            *pairs,
            *([dma((2,))] * 2),
            *([dma((1,))] * 2),
            *([dma((2,))] * 2),
            *([dma((half + 1,))] * 2),
        ],
        compiler_params=pltpu.CompilerParams(
            collective_id=0, has_side_effects=True, vmem_limit_bytes=32 << 20
        ),
        name="radial_attention",
    )(stay(block_list), stay(block_count), timestep, *map(stay, arrays))


def solution(mesh, chunk=4):
    return jax.shard_map(
        functools.partial(shards, chunk=chunk),
        mesh=mesh,
        in_specs=(
            P("net", "tm", "space", None, None),
            P("net", "tm", "space", None, None),
            P("net", "tm", "space", None, None),
            P("net", None, None),
            P("tm", "space", None),
            P("tm", "space"),
            P(),
        ),
        out_specs=P("tm", "space", None, "net"),
        check_vma=False,
    )
```

```python
import functools
import math

import jax
import jax.numpy as jnp
from jax import lax
from jax.experimental import pallas as pl
from jax.experimental.pallas import tpu as pltpu
from jax.sharding import PartitionSpec as P

HD = 128
FREQ = 256
DEAD = -1e30
RATE = HD**-0.5 * math.log2(math.e)
MESH = pl.DeviceIdType.MESH
LINES = 4
AHEAD = 3


def kernel(
    chunk,
    list_in,
    count_in,
    time_in,
    q_in,
    k_in,
    v_in,
    proj_in,
    out,
    block_list,
    block_count,
    timestep,
    queries,
    keys,
    values,
    proj,
    gate,
    bias,
    bias_in,
    bias_out,
    own_mix,
    own_stat,
    columns,
    scales,
    far_mix,
    far_stat,
    back_mix,
    back_stat,
    few_mix,
    share_out,
    share_in,
    pair_out,
    pair_in,
    both_out,
    both_in,
    net_out,
    net_in,
    local_sem,
    bias_send,
    bias_recv,
    q_send,
    q_recv,
    k_send,
    k_recv,
    v_send,
    v_recv,
    mix_send,
    mix_recv,
    stat_send,
    stat_recv,
    share_send,
    share_recv,
    pair_send,
    pair_recv,
    both_send,
    both_recv,
    net_send,
    net_recv,
):
    block_len, features = q_in.shape[-2:]
    heads = features // HD
    kept = heads // 2
    few = chunk // 2
    half = (kept - few) // chunk
    steps = 1 + 2 * half
    width = chunk * HD
    rows = 2 * block_len
    frames, spaces = lax.axis_size("tm"), lax.axis_size("space")
    frame, space, net = lax.axis_index("tm"), lax.axis_index("space"), lax.axis_index("net")
    down, has_down = {"tm": frame - 1}, frame > 0
    up, has_up = {"tm": frame + 1}, frame < frames - 1
    left, has_left = {"space": space - 1}, space > 0
    right, has_right = {"space": space + 1}, space < spaces - 1
    other = {"net": 1 - net}

    barrier = pltpu.get_barrier_semaphore()
    peers = ((down, has_down), (up, has_up), (left, has_left), (right, has_right))
    for peer, there in peers:

        @pl.when(there)
        def _():
            pl.semaphore_signal(barrier, inc=1, device_id=peer, device_id_type=MESH)

    pl.semaphore_signal(barrier, inc=1, device_id=other, device_id_type=MESH)

    tables = [
        pltpu.make_async_copy(list_in, block_list, local_sem.at[8]),
        pltpu.make_async_copy(count_in, block_count, local_sem.at[9]),
        pltpu.make_async_copy(time_in, timestep, local_sem.at[10]),
    ]
    for copy in tables:
        copy.start()
    own_copies = [
        pltpu.make_async_copy(q_in.at[0, 0], queries.at[pl.ds(2, 2)], local_sem.at[0]),
        pltpu.make_async_copy(k_in.at[0, 0], keys.at[pl.ds(1, 2)], local_sem.at[1]),
        pltpu.make_async_copy(v_in.at[0, 0], values.at[pl.ds(1, 2)], local_sem.at[2]),
        pltpu.make_async_copy(proj_in.at[0], proj, local_sem.at[3]),
    ]
    for copy in own_copies:
        copy.start()

    for copy in tables:
        copy.wait()

    column = lax.broadcasted_iota(jnp.int32, (2, 4 * block_len), 1) // block_len
    sublane = lax.broadcasted_iota(jnp.int32, (2, 4 * block_len), 0)
    slots = block_list.shape[-1]

    def listed(row, frame_step, block_step):
        wanted = (frame + frame_step) * (2 * spaces) + 2 * space + row + block_step
        found = jnp.int32(0)
        for slot in range(slots):
            hit = (block_list[0, row, slot] == wanted) & (slot < block_count[0, row])
            found = found | hit.astype(jnp.int32)
        return jnp.where(found > 0, jnp.float32(0.0), jnp.float32(DEAD))

    def bias_rows(frame_step):
        both = []
        for row in range(2):
            entries = jnp.full(column.shape, DEAD, jnp.float32)
            for place in range(row, row + 3):
                entry = listed(row, frame_step, place - 1 - row)
                entries = jnp.where(column == place, entry, entries)
            both.append(entries)
        return jnp.where(sublane == 0, both[0], both[1])

    bias_out[0] = bias_rows(-1)
    bias_out[1] = bias_rows(1)
    bias_in[1] = bias_rows(0)

    pl.semaphore_wait(barrier, 1 + sum(there.astype(jnp.int32) for _, there in peers))

    def send(src, dst, send_sem, recv_sem, peer):
        return pltpu.make_async_remote_copy(
            src_ref=src,
            dst_ref=dst,
            send_sem=send_sem,
            recv_sem=recv_sem,
            device_id=peer,
            device_id_type=MESH,
        )

    theirs, ours = (1 - net) * kept * HD, net * kept * HD

    def offset_of(step):
        return few * HD + lax.rem(step - 1, half) * width

    def first_lane(step):
        return jnp.where(step <= half, theirs, ours) + offset_of(step)

    def pieces(step):
        if isinstance(step, int) and step == 0:
            return [
                (number, pl.ds(pl.multiple_of(start, HD), few * HD))
                for number, start in ((0, theirs), (steps, ours))
            ]
        return [(step, pl.ds(pl.multiple_of(first_lane(step), HD), width))]

    def head_lanes(step, j):
        if isinstance(step, int) and step == 0:
            start = theirs + j * HD if j < few else ours + (j - few) * HD
        else:
            start = first_lane(step) + j * HD
        return pl.ds(pl.multiple_of(start, HD), HD)

    def half_lanes(step, j=None):
        if isinstance(step, int) and step == 0:
            return pl.ds(0, few * HD) if j is None else pl.ds(j * HD, HD)
        if j is None:
            return pl.ds(pl.multiple_of(offset_of(step), HD), width)
        return pl.ds(pl.multiple_of(offset_of(step) + j * HD, HD), HD)

    over_z = ((0, down, 2, has_down, has_up), (1, up, 0, has_up, has_down))
    over_space = ((0, left, 3, has_left, has_right), (1, right, 0, has_right, has_left))

    def bias_copies():
        return [
            (
                send(
                    bias_out.at[way], bias_in.at[group], bias_send.at[way], bias_recv.at[way], peer
                ),
                sends,
                receives,
            )
            for way, peer, group, sends, receives in over_z
        ]

    def query_copies(step):
        return [
            (
                send(
                    q_in.at[0, 0, :, :, at],
                    queries.at[pl.ds(2 * group, 2), :, at],
                    q_send.at[number, way],
                    q_recv.at[number, way],
                    peer,
                ),
                sends,
                receives,
            )
            for number, at in pieces(step)
            for way, peer, group, sends, receives in over_z
        ]

    def key_copies(step):
        return [
            (
                send(
                    source.at[0, 0, way, :, at],
                    held.at[slot, :, at],
                    send_sem.at[number, way],
                    recv_sem.at[number, way],
                    peer,
                ),
                sends,
                receives,
            )
            for number, at in pieces(step)
            for source, held, send_sem, recv_sem in (
                (k_in, keys, k_send, k_recv),
                (v_in, values, v_send, v_recv),
            )
            for way, peer, slot, sends, receives in over_space
        ]

    def returning(far, back, send_sem, recv_sem):
        return [
            (
                send(far.at[way], back.at[1 - way], send_sem.at[way], recv_sem.at[way], peer),
                sends,
                receives,
            )
            for way, peer, _, sends, receives in over_z
        ]

    def share_copies():
        return returning(share_out, share_in, share_send, share_recv)

    def both_copies():
        return returning(both_out, both_in, both_send, both_recv)

    def pair_copy():
        return send(pair_out, pair_in, pair_send.at[0], pair_recv.at[0], other)

    def stat_returns(step):
        return [
            (
                send(
                    far_stat.at[step, way],
                    back_stat.at[step, 1 - way],
                    stat_send.at[step, way],
                    stat_recv.at[step, way],
                    peer,
                ),
                sends,
                receives,
            )
            for way, peer, _, sends, receives in over_z
        ]

    def mix_returns(step, part=None):
        [(number, at)] = pieces(step)
        if part is not None:
            number = (steps - 1, steps)[part]
            at = pl.ds(pl.multiple_of(first_lane(step) + part * few * HD, HD), few * HD)
        return [
            (
                send(
                    far_mix.at[way, :, at],
                    back_mix.at[1 - way, :, at],
                    mix_send.at[number, way],
                    mix_recv.at[number, way],
                    peer,
                ),
                sends,
                receives,
            )
            for way, peer, _, sends, receives in over_z
        ]

    def crossing(step):
        at = half_lanes(step)
        return send(
            net_out.at[:, at], net_in.at[:, at], net_send.at[step], net_recv.at[step], other
        )

    def start_all(copies):
        for copy, sends, _ in copies:
            pl.when(sends)(copy.start)

    def receive_all(copies):
        for copy, _, receives in copies:
            pl.when(receives)(copy.wait_recv)

    def sent_all(copies):
        for copy, sends, _ in copies:
            pl.when(sends)(copy.wait_send)

    start_all(bias_copies())

    start_all(query_copies(0) + key_copies(0))
    for step in range(1, AHEAD):
        start_all(query_copies(step))

    @pl.loop(1, steps)
    def _(step):
        start_all(key_copies(step))

    def edge_copies(block, place):
        return [
            pltpu.make_async_copy(k_in.at[0, 0, block], keys.at[place], local_sem.at[4 + block]),
            pltpu.make_async_copy(v_in.at[0, 0, block], values.at[place], local_sem.at[6 + block]),
        ]

    edges = ((has_left, 0, 0), (has_right, 1, 3))
    for there, block, place in edges:

        @pl.when(jnp.logical_not(there))
        def _():
            for copy in edge_copies(block, place):
                copy.start()

    for there, way in ((has_down, 0), (has_up, 1)):

        @pl.when(jnp.logical_not(there))
        def _():
            for block in range(2):
                queries[4 * way + block] = jnp.zeros((block_len, features), queries.dtype)
            bias_in[2 * way] = jnp.full(bias_in.shape[1:], DEAD, jnp.float32)
            back_mix[way] = jnp.zeros(back_mix.shape[1:], back_mix.dtype)
            for step in range(steps):
                back_stat[step, way] = jnp.full(back_stat.shape[2:], DEAD, jnp.float32)
            share_in[way] = jnp.zeros(share_in.shape[1:], jnp.float32)
            both_in[way] = jnp.zeros(both_in.shape[1:], both_in.dtype)

    order = lax.broadcasted_iota(jnp.int32, (8, FREQ // 2), 1).astype(jnp.float32)
    rates = jnp.exp(-jnp.log(jnp.full_like(order, 10000.0)) * order / (FREQ // 2))
    angle = timestep[0].astype(jnp.float32) * rates
    feature = jnp.concatenate([jnp.cos(angle), jnp.sin(angle)], axis=1)
    feature = (feature / (1.0 + jnp.exp(-feature))).astype(jnp.bfloat16)
    polarity = 2.0 * net.astype(jnp.float32) - 1.0
    for copy in own_copies:
        copy.wait()
    for there, block, place in edges:

        @pl.when(jnp.logical_not(there))
        def _():
            for copy in edge_copies(block, place):
                copy.wait()

    columns[...] = jnp.zeros_like(columns)
    receive_all(bias_copies())
    for group in range(3):
        for row in range(2):
            bias[2 * group + row] = jnp.broadcast_to(
                bias_in[group, row : row + 1, :], bias.shape[1:]
            )

    def attend(step):
        receive_all(query_copies(step) + key_copies(step))
        for j in range(chunk):
            at = head_lanes(step, j)
            q = queries[:, :, at].reshape(6 * block_len, HD)
            k = keys[:, :, at].reshape(4 * block_len, HD)
            v = values[:, :, at].reshape(4 * block_len, HD)
            scores = lax.dot_general(
                q, k, (((1,), (1,)), ((), ())), preferred_element_type=jnp.float32
            )
            scores = scores.reshape(6, block_len // 8, 8, 4 * block_len) + bias[...][:, None]
            scores = scores.reshape(6 * block_len, 4 * block_len)
            top = jnp.max(scores, axis=-1, keepdims=True)
            expo = jnp.exp2((scores - top) * RATE)
            total = jnp.sum(expo, axis=-1, keepdims=True)
            weight = top * RATE + jnp.log2(total)
            mix = jnp.dot(expo.astype(jnp.bfloat16), v, preferred_element_type=jnp.float32)
            mix = mix * (1.0 / total)
            for group in range(3):
                part = slice(group * rows, (group + 1) * rows)
                columns[group, :, j : j + 1] = weight[part]
            own_mix[:, at] = mix[rows : 2 * rows]
            for way, part in ((0, mix[:rows]), (1, mix[2 * rows :])):
                if isinstance(step, int) and step == 0:
                    few_mix[way, :, j * HD : (j + 1) * HD] = part
                else:
                    far_mix[way, :, at] = part.astype(jnp.bfloat16)
        far_stat[step, 0] = columns[0].T[:LINES]
        own_stat[step] = columns[1].T[:LINES]
        far_stat[step, 1] = columns[2].T[:LINES]
        start_all(stat_returns(step))

    def shares_of(step):
        receive_all(stat_returns(step))
        weights = [own_stat[step], back_stat[step, 0], back_stat[step, 1]]
        top = functools.reduce(jnp.maximum, weights)
        shares = [jnp.exp2(weight - top) for weight in weights]
        whole = 1.0 / sum(shares)
        return [share * whole for share in shares]

    def upright(tiles):
        filler = jnp.zeros((8 - LINES, rows), jnp.float32)
        tiles = [piece for tile in tiles for piece in (tile, filler)]
        filler = jnp.zeros((HD - 4 * len(tiles), rows), jnp.float32)
        return jnp.concatenate([*tiles, filler], axis=0).T

    def gates_of(at):
        return jnp.broadcast_to(gate[:1, at], (rows, HD))

    def tell_shares():
        shares = shares_of(0)
        share_out[0] = shares[1]
        share_out[1] = shares[2]
        start_all(share_copies())
        share = upright(shares[:1])
        for j in range(chunk):
            at = head_lanes(0, j)
            own = own_mix[:, at] * (share[:, j : j + 1] * gates_of(at))
            if j < few:
                net_out[:, half_lanes(0, j)] = own.astype(jnp.bfloat16)
            else:
                own_mix[:, at] = own
        crossing(0).start()

    def exchange_halves():
        receive_all(share_copies())
        share = upright([share_in[0], share_in[1]])
        for way in range(2):
            for j in range(chunk):
                column = 8 * way + j
                here = pl.ds(j * HD, HD)
                part = few_mix[way, :, here] * (
                    share[:, column : column + 1] * gates_of(head_lanes(0, j))
                )
                if j < few:
                    pair_out[way, :, here] = part.astype(jnp.bfloat16)
                else:
                    few_mix[way, :, here] = part
        pair_copy().start()

    def return_sums():
        pair_copy().wait_recv()
        for way in range(2):
            both_out[way] = (
                few_mix[way, :, few * HD :] + pair_in[way].astype(jnp.float32)
            ).astype(jnp.bfloat16)
        start_all(both_copies())

    attend(0)

    @pl.loop(0, heads)
    def _(head):
        at = pl.ds(pl.multiple_of(head * HD, HD), HD)
        gate[:, at] = polarity * jnp.dot(
            feature, proj[:, at], preferred_element_type=jnp.float32
        )

    @pl.loop(1, steps)
    def _(step):
        @pl.when(step + AHEAD - 1 < steps)
        def _():
            start_all(query_copies(step + AHEAD - 1))

        attend(step)
        pl.when(step == 1)(tell_shares)

        @pl.when(step < steps - 1)
        def _():
            start_all(mix_returns(step))

        @pl.when(step == steps - 1)
        def _():
            start_all(mix_returns(steps - 1, 0) + mix_returns(steps - 1, 1))

        pl.when(step == 2)(exchange_halves)
        pl.when(step == min(3, steps - 1))(return_sums)

    def combine(step):
        shares = upright(shares_of(step))
        for j in range(chunk):
            at = head_lanes(step, j)
            gates = gates_of(at)
            own_mix[:, at] = own_mix[:, at] * (shares[:, j : j + 1] * gates)
            for way in range(2):
                column = 8 + 8 * way + j
                scales[way, j] = shares[:, column : column + 1] * gates

        def term(j):
            at = head_lanes(step, j)
            parts = [scales[way, j] * back_mix[way, :, at].astype(jnp.float32) for way in (0, 1)]
            return own_mix[:, at] + parts[0] + parts[1]

        @pl.when(step <= half)
        def _():
            receive_all(mix_returns(step))
            for j in range(chunk):
                net_out[:, half_lanes(step, j)] = term(j).astype(jnp.bfloat16)
            crossing(step).start()

        @pl.when(step > half)
        def _():
            crossing(step - half).wait_recv()
            last = isinstance(step, int) and step == steps - 1
            if not last:
                receive_all(mix_returns(step))
            for j in range(chunk):
                if last and j % few == 0:
                    receive_all(mix_returns(step, j // few))
                at = half_lanes(step, j)
                full = term(j) + net_in[:, at].astype(jnp.float32)
                out[0, :, :, at] = full.astype(jnp.bfloat16).reshape(2, block_len, HD)

    def combine_few():
        crossing(0).wait_recv()
        receive_all(both_copies())
        for j in range(few):
            at = half_lanes(0, j)
            full = own_mix[:, head_lanes(0, few + j)] + net_in[:, at].astype(jnp.float32)
            for way in range(2):
                full = full + both_in[way, :, at].astype(jnp.float32)
            out[0, :, :, at] = full.astype(jnp.bfloat16).reshape(2, block_len, HD)

    pl.loop(1, steps - 1)(combine)
    combine_few()

    sent_all(bias_copies() + query_copies(0) + key_copies(0) + stat_returns(0))

    @pl.loop(1, steps)
    def _(step):
        sent_all(query_copies(step) + key_copies(step) + stat_returns(step))

    sent_all(share_copies() + both_copies())
    pair_copy().wait_send()
    for step in range(half + 1):
        crossing(step).wait_send()

    @pl.loop(1, steps - 1)
    def _(step):
        sent_all(mix_returns(step))

    combine(steps - 1)
    sent_all(mix_returns(steps - 1, 0) + mix_returns(steps - 1, 1))


def shards(query_rows, key_rows, value_rows, time_proj, block_list, block_count, timestep, *, chunk):
    block_len, features = query_rows.shape[-2:]
    heads = features // HD
    few = chunk // 2
    half = (heads // 2 - few) // chunk
    steps = 1 + 2 * half
    rows = 2 * block_len
    bf16, f32 = jnp.bfloat16, jnp.float32
    vmem, dma = pltpu.VMEM, pltpu.SemaphoreType.DMA
    hbm = pl.BlockSpec(memory_space=pltpu.HBM)
    arrays = (query_rows, key_rows, value_rows, time_proj)

    def stay(array):
        return pltpu.with_memory_space_constraint(array, pltpu.HBM)

    pairs = [dma((steps, 2))] * 2
    pieces = [dma((steps + 1, 2))] * 2
    return pl.pallas_call(
        functools.partial(kernel, chunk),
        out_shape=jax.ShapeDtypeStruct((1, 2, block_len, features // 2), bf16),
        in_specs=[hbm] * 7,
        out_specs=pl.BlockSpec(memory_space=pltpu.VMEM),
        scratch_shapes=[
            pltpu.SMEM(block_list.shape, jnp.int32),
            pltpu.SMEM(block_count.shape, jnp.int32),
            pltpu.SMEM(timestep.shape, jnp.int32),
            vmem((6, block_len, features), bf16),
            vmem((4, block_len, features), bf16),
            vmem((4, block_len, features), bf16),
            vmem((FREQ, features), bf16),
            vmem((8, features), f32),
            vmem((6, 8, 4 * block_len), f32),
            vmem((3, 2, 4 * block_len), f32),
            vmem((2, 2, 4 * block_len), f32),
            vmem((rows, features), f32),
            vmem((steps, LINES, rows), f32),
            vmem((3, rows, HD), f32),
            vmem((2, chunk, rows, HD), f32),
            vmem((2, rows, features), bf16),
            vmem((steps, 2, LINES, rows), f32),
            vmem((2, rows, features), bf16),
            vmem((steps, 2, LINES, rows), f32),
            vmem((2, rows, chunk * HD), f32),
            *([vmem((2, LINES, rows), f32)] * 2),
            *([vmem((2, rows, few * HD), bf16)] * 2),
            *([vmem((2, rows, few * HD), bf16)] * 2),
            vmem((rows, features // 2), bf16),
            vmem((rows, features // 2), bf16),
            dma((11,)),
            *([dma((2,))] * 2),
            *pieces,
            *pieces,
            *pieces,
            *pieces,
            *pairs,
            *([dma((2,))] * 2),
            *([dma((1,))] * 2),
            *([dma((2,))] * 2),
            *([dma((half + 1,))] * 2),
        ],
        compiler_params=pltpu.CompilerParams(
            collective_id=0, has_side_effects=True, vmem_limit_bytes=32 << 20
        ),
        name="radial_attention",
    )(stay(block_list), stay(block_count), timestep, *map(stay, arrays))


def solution(mesh, chunk=4):
    return jax.shard_map(
        functools.partial(shards, chunk=chunk),
        mesh=mesh,
        in_specs=(
            P("net", "tm", "space", None, None),
            P("net", "tm", "space", None, None),
            P("net", "tm", "space", None, None),
            P("net", None, None),
            P("tm", "space", None),
            P("tm", "space"),
            P(),
        ),
        out_specs=P("tm", "space", None, "net"),
        check_vma=False,
    )
```
